32 devices in a mesh: depth: 4 (over y, core), lat: 8 (over z, x).
Axes of the slice: x: 2, y: 2, z: 4, core: 2. Of those that a mesh axis runs over, the one named last changes fastest.
Arguments:
- fields: float32 [4, 2, 2, 2, 512, 512], P('depth', None, None, None, 'lat'), may hold values from -6 to 6
- surface: float32 [2, 2, 2, 512, 512], P(None, None, None, 'lat'), may hold values from -6 to 6
- held_freqs: int32 [4, 2], P('depth'), may hold values from 8 to 63
- surface_freqs: int32 [2], replicated, may hold values from 8 to 63
- ref_slowness: float32 [4, 1, 2], P('depth'), may hold values from 0.6 to 1.2
- weights: float32 [4, 1, 512, 512], P('depth', None, 'lat'), may hold values from 0 to 1
- regions: int32 [4, 1, 512, 512], P('depth', None, 'lat'), may hold values from 0 to 7
- region_slowness: float32 [4, 1, 8], P('depth'), may hold values from 0.6 to 1.2
Outputs:
- fields_out: float32 [4, 2, 2, 2, 512, 512], P('depth', None, None, None, 'lat')
- image_out: float32 [4, 1, 16, 512, 512], P('depth', None, None, 'lat')
The draws below stay inside these ranges and needn't reach their ends.
All inputs are finite; a program needn't handle non-finite values.
Results may differ from the reference program's by a relative error of at most 0.0003.
Values sent between devices are 32-bit elements; how exact they have to be, the bound alone decides.
A program may use at most 64 MiB of HBM per device.

```python
import math
import jax
import jax.numpy as jnp
from jax import lax

NX = 512
NY = 512
FREQ = 2
LEVELS = 1
LAGS = 16
REGIONS = 8
SECTIONS = 4


def plant(drawn, stream_key, low, top_value):
    index_at = [jax.random.randint(jax.random.fold_in(stream_key, axis), (), 0, length) for axis, length in enumerate(drawn.shape)]
    main_axis = drawn.shape.index(max(drawn.shape))
    next_to = index_at[:main_axis] + [(index_at[main_axis] + 1) % drawn.shape[main_axis]] + index_at[main_axis + 1:]
    return drawn.at[tuple(index_at)].set(low).at[tuple(next_to)].set(top_value)


def shard_levels(key, dims, pieces, least, top_value):
    loudness, own = 1.0, jax.random.fold_in(key, 6)
    for axis_at, shards_of in pieces:
        heights = jnp.exp(jax.random.uniform(jax.random.fold_in(own, axis_at), (shards_of,), jnp.float32, least / len(pieces), top_value / len(pieces)))
        loudness = loudness * jnp.repeat(heights, dims[axis_at] // shards_of).reshape([-1 if axis == axis_at else 1 for axis in range(len(dims))])
    return loudness


def centred(stream_key, dims, width, reach, cuts=(), kind=jnp.bfloat16):
    result = width * jax.random.normal(stream_key, dims, jnp.float32)
    if cuts:
        result = result * shard_levels(stream_key, dims, cuts, -0.22, 0.18)
    return jnp.clip(result, -reach, reach).astype(kind)


def setup_inputs(seed: int = 0) -> dict:
    keys = jax.random.split(jax.random.key(seed), 9)
    return {
        "fields": centred(keys[0], (SECTIONS, 2, 2, FREQ, NX, NY), 1.0, 6.0, ((0, 4), (4, 8)), jnp.float32),
        "surface": centred(keys[1], (2, 2, FREQ, NX, NY), 1.0, 6.0, ((3, 8),), jnp.float32),
        "held_freqs": plant(jax.random.randint(keys[2], (SECTIONS, FREQ), 8, 64), jax.random.fold_in(keys[2], 1), 8, 63).astype(jnp.int32),
        "surface_freqs": jax.random.randint(keys[3], (FREQ,), 8, 64).astype(jnp.int32),
        "ref_slowness": jnp.clip(0.6 + 0.6 * jax.random.uniform(keys[4], (SECTIONS, LEVELS, 2), jnp.float32) ** shard_levels(keys[4], (SECTIONS, LEVELS, 2), ((0, 4),), -0.2, 0.2), 0.6, 1.2),
        "weights": jnp.clip(1.0 * jax.random.uniform(keys[5], (SECTIONS, LEVELS, NX, NY), jnp.float32) ** shard_levels(keys[5], (SECTIONS, LEVELS, NX, NY), ((0, 4), (2, 8)), -0.2, 0.2), 0.0, 1.0),
        "regions": plant(jax.random.randint(keys[6], (SECTIONS, LEVELS, NX, NY), 0, REGIONS), jax.random.fold_in(keys[6], 1), 0, REGIONS - 1).astype(jnp.int32),
        "region_slowness": jnp.clip(0.6 + 0.6 * jax.random.uniform(keys[7], (SECTIONS, LEVELS, REGIONS), jnp.float32) ** shard_levels(keys[7], (SECTIONS, LEVELS, REGIONS), ((0, 4),), -0.2, 0.2), 0.6, 1.2),
    }


omega_step = 0.04
depth_step = 1.0

def wave_numbers(length):
    positions = jnp.arange(length, dtype=jnp.int32)
    folded = jnp.where(positions < length // 2, positions, positions - length)
    return folded.astype(jnp.float32) * (2.0 * math.pi / length)

def level_step(wave_field, omega_batch, slow_pair, weight, cell_slow, sign_pair):
    wave_x = wave_numbers(NX)
    wave_y = wave_numbers(NY)
    squared = wave_x[:, None] ** 2 + wave_y[None, :] ** 2
    spectrum = jnp.fft.fft2(wave_field, axes=(-2, -1))
    ref_fields = []
    for ref_index in range(2):
        wave_base = omega_batch[:, None, None] * slow_pair[ref_index]
        wave_gap = wave_base * wave_base - squared[None]
        amplitude = jnp.exp(-jnp.sqrt(jnp.maximum(-wave_gap, 0.0)) * depth_step)
        turning = sign_pair[:, None, None, None] * jnp.sqrt(jnp.maximum(wave_gap, 0.0))[None] * depth_step
        factor = lax.complex(amplitude[None] * jnp.cos(turning), amplitude[None] * jnp.sin(turning))
        ref_fields.append(jnp.fft.ifft2(spectrum * factor, axes=(-2, -1)))
    mixed_field = weight * ref_fields[0] + (1.0 - weight) * ref_fields[1]
    blend_slow = weight * slow_pair[0] + (1.0 - weight) * slow_pair[1]
    lens_angle = sign_pair[:, None, None, None] * omega_batch[None, :, None, None] * (cell_slow - blend_slow)[None, None] * depth_step
    return mixed_field * lax.complex(jnp.cos(lens_angle), jnp.sin(lens_angle))

def image_terms(wave_field):
    half_lags = LAGS // 2
    row_count = wave_field.shape[-2]
    source = jnp.pad(wave_field[0], ((0, 0), (half_lags, half_lags), (0, 0)))
    receiver = jnp.pad(wave_field[1], ((0, 0), (half_lags, half_lags), (0, 0)))
    lag_terms = []
    for lag_index in range(LAGS):
        offset = lag_index - half_lags
        source_rows = source[:, half_lags - offset:half_lags - offset + row_count]
        receiver_rows = receiver[:, half_lags + offset:half_lags + offset + row_count]
        product = jnp.real(source_rows) * jnp.real(receiver_rows) + jnp.imag(source_rows) * jnp.imag(receiver_rows)
        lag_terms.append(lax.optimization_barrier(jnp.sum(product, axis=0)))
    return jnp.stack(lag_terms)

def reference(fields, surface, held_freqs, surface_freqs, ref_slowness, weights, regions, region_slowness):
    sign_pair = jnp.array([-1.0, 1.0], dtype=jnp.float32)
    sections = fields.shape[0]
    held_waves = [lax.complex(fields[section, 0], fields[section, 1]) for section in range(sections)]
    omegas = [held_freqs[section].astype(jnp.float32) * omega_step for section in range(sections)]
    cells = [[jnp.take(region_slowness[section, level_index], regions[section, level_index]) for level_index in range(LEVELS)] for section in range(sections)]
    images = [[None for level_index in range(LEVELS)] for section in range(sections)]
    results = []
    for tick_index in range(2):
        results = []
        for section in range(sections):
            wave_field = held_waves[section]
            for level_index in range(LEVELS):
                wave_field = level_step(wave_field, omegas[section], ref_slowness[section, level_index], weights[section, level_index], cells[section][level_index], sign_pair)
                lag_term = image_terms(wave_field)
                if tick_index == 0:
                    images[section][level_index] = lag_term
                else:
                    images[section][level_index] = images[section][level_index] + lag_term
            results.append(wave_field)
        if tick_index == 0:
            held_waves = [lax.complex(surface[0], surface[1])] + results[:-1]
            omegas = [surface_freqs.astype(jnp.float32) * omega_step] + omegas[:-1]
    fields_out = jnp.stack([jnp.stack([jnp.real(wave_field), jnp.imag(wave_field)]) for wave_field in results])
    image_out = jnp.stack([jnp.stack(images[section]) for section in range(sections)])
    return (fields_out, image_out)
```

```python
import functools
import math

import jax
import jax.numpy as jnp
import ml_dtypes
import numpy as np
from jax import lax
from jax.experimental import pallas as pl
from jax.experimental.pallas import tpu as pltpu
from jax.sharding import PartitionSpec as P

LAGS = 16
REGIONS = 8


omega_step = 0.04
depth_step = 1.0
exact_math = lax.Precision.HIGHEST


def with_halo(cells, sides, width):
    for axis, dim in sides:
        count = lax.axis_size(axis)
        ends = count - 1
        head = lax.slice_in_dim(cells, 0, width, axis=dim)
        tail = lax.slice_in_dim(cells, cells.shape[dim] - width, cells.shape[dim], axis=dim)
        cells = jnp.concatenate(
            [
                lax.ppermute(tail, axis, [(i, (i + 1) % count) for i in range(ends)]),
                cells,
                lax.ppermute(head, axis, [((i + 1) % count, i) for i in range(ends)]),
            ],
            axis=dim,
        )
    return cells


def passed_along(value, axis, steps):
    count = lax.axis_size(axis)
    leading, last = (max(0, -steps), min(count, count - steps))
    return lax.ppermute(value, axis, [(source, source + steps) for source in range(leading, last)])


def factor_pair(length):
    first_len = 1
    for divisor in range(1, math.isqrt(length) + 1):
        if length % divisor == 0:
            first_len = divisor
    return (first_len, length // first_len)


def unit_phase(product_index, period, direction):
    turning = direction * 2.0 * math.pi / period * product_index.astype(jnp.float32)
    return (jnp.cos(turning), jnp.sin(turning))


def transform_tables(first_len, second_len, direction):
    first_range = jnp.arange(first_len, dtype=jnp.int32)
    second_range = jnp.arange(second_len, dtype=jnp.int32)
    outer_table = unit_phase(
        first_range[:, None] * first_range[None, :] % first_len, first_len, direction
    )
    twist_table = unit_phase(
        first_range[:, None] * second_range[None, :] % (first_len * second_len),
        first_len * second_len,
        direction,
    )
    inner_table = unit_phase(
        second_range[:, None] * second_range[None, :] % second_len, second_len, direction
    )
    return (outer_table, twist_table, inner_table)


def complex_product(pattern, values, table_pair):
    real_times = jnp.einsum(pattern, values[0], table_pair[0], precision=exact_math)
    imag_times = jnp.einsum(pattern, values[1], table_pair[1], precision=exact_math)
    joint_times = jnp.einsum(
        pattern, values[0] + values[1], table_pair[0] + table_pair[1], precision=exact_math
    )
    return jnp.stack([real_times - imag_times, joint_times - real_times - imag_times])


def complex_scale(values, factor):
    return jnp.stack(
        [
            values[0] * factor[0] - values[1] * factor[1],
            values[0] * factor[1] + values[1] * factor[0],
        ]
    )


def wave_numbers(positions, length):
    folded = jnp.where(positions < length // 2, positions, positions - length)
    return folded.astype(jnp.float32) * (2.0 * math.pi / length)


def forward_rows(values, tables, lane_count):
    groups, row_count, col_count = (values.shape[1], values.shape[2], values.shape[3])
    outer_table, twist_table, inner_table = tables
    split_first = outer_table[0].shape[0]
    split_second = inner_table[0].shape[0]
    shaped = values.reshape(2, groups, row_count, split_first, split_second)
    segmented = complex_product("grjm,kj->gkmr", shaped, outer_table)
    segmented = complex_scale(segmented, (twist_table[0][:, :, None], twist_table[1][:, :, None]))
    segmented = complex_product("gkmr,lm->gklr", segmented, inner_table)
    return segmented.reshape(2, groups, lane_count, col_count * row_count // lane_count)


def forward_columns(values, tables, lane_count, col_block, row_count):
    groups = values.shape[1]
    outer_table, twist_table, inner_table = tables
    shaped = values.reshape(2, groups, lane_count, col_block, row_count)
    segmented = complex_product("gscr,ks->gkcr", shaped, outer_table)
    segmented = complex_scale(segmented, (twist_table[0][:, None, :], twist_table[1][:, None, :]))
    segmented = complex_product("gkcr,lr->gckl", segmented, inner_table)
    return segmented.reshape(2, groups, col_block, lane_count * row_count)


def inverse_columns(values, tables, lane_count, row_count):
    groups, col_block = (values.shape[1], values.shape[2])
    outer_table, twist_table, inner_table = tables
    shaped = values.reshape(2, groups, col_block, lane_count, row_count)
    segmented = complex_product("gckl,lr->gckr", shaped, inner_table)
    segmented = complex_scale(segmented, twist_table)
    segmented = complex_product("gckr,ks->gscr", segmented, outer_table)
    return segmented.reshape(2, groups, lane_count, col_block * row_count)


def inverse_rows(values, tables, depth_rows):
    groups = values.shape[1]
    outer_table, twist_table, inner_table = tables
    split_first = outer_table[0].shape[0]
    split_second = inner_table[0].shape[0]
    shaped = values.reshape(2, groups, split_first, split_second, depth_rows)
    segmented = complex_product("gklr,lm->gkmr", shaped, inner_table)
    segmented = complex_scale(segmented, (twist_table[0][:, :, None], twist_table[1][:, :, None]))
    segmented = complex_product("gkmr,kj->grjm", segmented, outer_table)
    return segmented.reshape(2, groups, depth_rows, split_first * split_second)


def level_step(
    wave_state, omega_batch, slow_pair, weight_rows, cell_rows, squared, tables_y, tables_x, layout
):
    lane_count, row_count, col_block, margin = layout
    freq_count = wave_state.shape[2]
    col_count = wave_state.shape[4]
    sign_pair = jnp.array([-1.0, 1.0], jnp.float32)
    flat_state = wave_state.reshape(2, 2 * freq_count, row_count, col_count)
    spectra = forward_rows(flat_state, tables_y[0], lane_count)
    spectra = lax.all_to_all(spectra, "lat", split_axis=2, concat_axis=2, tiled=True)
    spectra = forward_columns(spectra, tables_x[0], lane_count, col_block, row_count)
    spectra = spectra.reshape(2, 2, freq_count, col_block, lane_count * row_count)
    wave_base = omega_batch[None, :, None, None] * slow_pair[:, None, None, None]
    wave_gap = wave_base * wave_base - squared[None, None]
    amplitude = jnp.exp(-jnp.sqrt(jnp.maximum(-wave_gap, 0.0)) * depth_step)
    turning = (
        sign_pair[None, :, None, None, None]
        * jnp.sqrt(jnp.maximum(wave_gap, 0.0))[:, None]
        * depth_step
    )
    factor = (amplitude[:, None] * jnp.cos(turning), amplitude[:, None] * jnp.sin(turning))
    shifted = complex_scale(spectra[:, None], factor)
    shifted = shifted.reshape(2, 4 * freq_count, col_block, lane_count * row_count)
    returned = inverse_columns(shifted, tables_x[1], lane_count, row_count)
    returned = lax.all_to_all(returned, "lat", split_axis=2, concat_axis=2, tiled=True)
    depth_rows = row_count + 2 * margin
    ref_fields = inverse_rows(returned, tables_y[1], depth_rows)
    ref_fields = ref_fields.reshape(2, 2, 2, freq_count, depth_rows, col_count) * (
        1.0 / (lane_count * row_count * col_count)
    )
    mixed_field = weight_rows * ref_fields[:, 0] + (1.0 - weight_rows) * ref_fields[:, 1]
    blend_slow = weight_rows * slow_pair[0] + (1.0 - weight_rows) * slow_pair[1]
    lens_angle = (
        sign_pair[:, None, None, None]
        * omega_batch[None, :, None, None]
        * (cell_rows - blend_slow)[None, None]
        * depth_step
    )
    return complex_scale(mixed_field, (jnp.cos(lens_angle), jnp.sin(lens_angle)))


def lag_products(padded, half_lags, row_count):
    lag_terms = []
    for lag_index in range(2 * half_lags):
        offset = lag_index - half_lags
        source_rows = padded[:, 0, :, half_lags - offset : half_lags - offset + row_count]
        receiver_rows = padded[:, 1, :, half_lags + offset : half_lags + offset + row_count]
        lag_terms.append(jnp.sum(source_rows * receiver_rows, axis=(0, 1)))
    return jnp.stack(lag_terms)


def shards(
    fields, surface, held_freqs, surface_freqs, ref_slowness, weights, regions, region_slowness
):
    lane_count = lax.axis_size("lat")
    row_count = fields.shape[4]
    col_count = fields.shape[5]
    col_block = col_count // lane_count
    total_rows = lane_count * row_count
    half_lags = LAGS // 2
    split_first, split_second = factor_pair(col_count)
    tables_y = (
        transform_tables(split_first, split_second, -1.0),
        transform_tables(split_first, split_second, 1.0),
    )
    tables_x = (
        transform_tables(lane_count, row_count, -1.0),
        transform_tables(lane_count, row_count, 1.0),
    )
    block_index = lax.axis_index("lat")
    storage_y = block_index * col_block + jnp.arange(col_block, dtype=jnp.int32)
    index_y = storage_y // split_second + split_first * (storage_y % split_second)
    storage_x = jnp.arange(total_rows, dtype=jnp.int32)
    index_x = storage_x // row_count + lane_count * (storage_x % row_count)
    squared = (
        wave_numbers(index_y, col_count)[:, None] ** 2
        + wave_numbers(index_x, total_rows)[None, :] ** 2
    )
    region_ids = jnp.arange(REGIONS, dtype=jnp.int32)
    matches = (regions[0][None] == region_ids[:, None, None, None]).astype(jnp.float32)
    cell_slowness = jnp.sum(matches * jnp.transpose(region_slowness[0])[:, :, None, None], axis=0)
    margin = 0
    weight_rows_all = weights[0]
    layout = (lane_count, row_count, col_block, margin)
    wave_state = fields[0]
    omega_batch = held_freqs[0].astype(jnp.float32) * omega_step
    images = [jnp.zeros((LAGS, row_count, col_count), jnp.float32)]
    for tick_index in range(2):
        result = level_step(
            wave_state,
            omega_batch,
            ref_slowness[0, 0],
            weight_rows_all[0],
            cell_slowness[0],
            squared,
            tables_y,
            tables_x,
            layout,
        )
        wave_state = result
        padded = with_halo(result, (("lat", 3),), half_lags)
        images[0] = images[0] + lag_products(padded, half_lags, row_count)
        if tick_index == 0:
            moved, moved_omega = passed_along((wave_state, omega_batch), "depth", 1)
            at_top = lax.axis_index("depth") == 0
            wave_state = jnp.where(at_top, surface, moved)
            omega_batch = jnp.where(
                at_top, surface_freqs.astype(jnp.float32) * omega_step, moved_omega
            )
    return (wave_state[None], jnp.stack(images)[None])

def split_halves(value):
    high = value.astype(jnp.bfloat16)
    low = (value - high.astype(jnp.float32)).astype(jnp.bfloat16)
    return (high, low)


def dft_tables(length):
    index = np.arange(length)
    turning = 2.0 * np.pi / length * (index[:, None] * index[None, :] % length)
    tables = []
    for exact in (np.cos(turning), np.sin(turning)):
        high = exact.astype(ml_dtypes.bfloat16)
        low = (exact - high.astype(np.float64)).astype(ml_dtypes.bfloat16)
        tables += [high, low]
    return np.stack(tables)


def dot(left, right):
    return jnp.dot(left, right, preferred_element_type=jnp.float32)


def three_pass_left(tables, which, high, low):
    table_high, table_low = (tables[2 * which], tables[2 * which + 1])
    return dot(table_high, high) + (dot(table_high, low) + dot(table_low, high))


def three_pass_right(tables, which, high, low):
    table_high, table_low = (tables[2 * which], tables[2 * which + 1])
    return dot(high, table_high) + (dot(low, table_high) + dot(high, table_low))


def dft_left(tables, values, direction):
    half = values.shape[1] // 2
    high, low = split_halves(values)
    even = three_pass_left(tables, 0, high, low)
    odd = three_pass_left(tables, 1, high, low)
    return (
        even[:, :half] - direction * odd[:, half:],
        even[:, half:] + direction * odd[:, :half],
    )


def dft_right(tables, values, direction):
    half = values.shape[0] // 2
    high, low = split_halves(values)
    even = three_pass_right(tables, 0, high, low)
    odd = three_pass_right(tables, 1, high, low)
    return (
        even[:half] - direction * odd[half:],
        even[half:] + direction * odd[:half],
    )


def spread_rows(core, tables, values, keep_ref, send_ref):
    half = values.shape[0] // 2
    real, imag = dft_left(tables, values, -1.0)
    both = jnp.concatenate([real, imag], axis=1)
    first, second = (both[:half], both[half:])
    at_first = core == 0
    keep_ref[...] = jnp.where(at_first, first, second)
    send_ref[...] = jnp.where(at_first, second, first)


def start_kernel(core_ref, blocks_ref, tables_ref, keep_ref, send_ref):
    spread_rows(core_ref[0], tables_ref, blocks_ref[...], keep_ref, send_ref)


def folded(positions, length):
    moved = jnp.where(positions < length // 2, positions, positions - length)
    return moved.astype(jnp.float32) * (2.0 * math.pi / length)


def middle_kernel(scale, core_ref, numbers_ref, own_ref, other_ref, tables_ref, keep_ref, send_ref):
    core = core_ref[0]
    at_first = core == 0
    rows, width = own_ref.shape
    half = width // 2
    own, other = (own_ref[...], other_ref[...])
    first = jnp.where(at_first, own, other)
    second = jnp.where(at_first, other, own)
    values = jnp.concatenate(
        [
            jnp.concatenate([first[:, :half], second[:, :half]], axis=1),
            jnp.concatenate([first[:, half:], second[:, half:]], axis=1),
        ],
        axis=0,
    )
    real, imag = dft_right(tables_ref, values, -1.0)
    kx = folded(lax.broadcasted_iota(jnp.int32, (rows, 1), 0) + core * rows, 2 * rows)
    ky = folded(lax.broadcasted_iota(jnp.int32, (1, width), 1), width)
    squared = kx * kx + ky * ky
    omega, sign = (numbers_ref[0], numbers_ref[1])
    for ref_index in range(2):
        base = omega * numbers_ref[2 + ref_index]
        gap = base * base - squared
        amplitude = jnp.exp(-jnp.sqrt(jnp.maximum(-gap, 0.0))) * scale
        turning = jnp.sqrt(jnp.maximum(gap, 0.0))
        cosine = amplitude * jnp.cos(turning)
        sine = amplitude * (sign * jnp.sin(turning))
        shifted = jnp.concatenate([real * cosine - imag * sine, real * sine + imag * cosine], axis=0)
        back_real, back_imag = dft_right(tables_ref, shifted, 1.0)
        first = jnp.concatenate([back_real[:, :half], back_imag[:, :half]], axis=1)
        second = jnp.concatenate([back_real[:, half:], back_imag[:, half:]], axis=1)
        keep_ref[ref_index] = jnp.where(at_first, first, second)
        send_ref[ref_index] = jnp.where(at_first, second, first)


def continued(core, numbers_ref, own_ref, other_ref, cells_ref, tables_ref):
    at_first = core == 0
    rows, width = own_ref.shape[1:]
    half = width // 2
    fields = []
    for ref_index in range(2):
        own, other = (own_ref[ref_index], other_ref[ref_index])
        values = jnp.concatenate(
            [jnp.where(at_first, own, other), jnp.where(at_first, other, own)], axis=0
        )
        fields.append(dft_left(tables_ref, values, 1.0))
    weight = cells_ref[:, 0].reshape(2 * rows, half)
    cell = cells_ref[:, 1].reshape(2 * rows, half)
    rest = 1.0 - weight
    real = weight * fields[0][0] + rest * fields[1][0]
    imag = weight * fields[0][1] + rest * fields[1][1]
    blend = weight * numbers_ref[2] + rest * numbers_ref[3]
    angle = numbers_ref[1] * numbers_ref[0] * (cell - blend)
    cosine, sine = (jnp.cos(angle), jnp.sin(angle))
    return jnp.concatenate([real * cosine - imag * sine, real * sine + imag * cosine], axis=1)


def put_blocks(values, blocks_ref):
    count, tall, width = blocks_ref.shape
    rows = values.shape[0] // count
    margin = (tall - rows) // 2
    edge = jnp.zeros((margin, width), jnp.float32)
    for block in range(count):
        start = block * rows
        blocks_ref[block, margin : margin + rows] = values[start : start + rows]
        blocks_ref[block, :margin] = values[start - margin : start] if block else edge
        after = start + rows
        blocks_ref[block, margin + rows :] = (
            values[after : after + margin] if block < count - 1 else edge
        )


def turn_kernel(
    core_ref,
    numbers_ref,
    own_ref,
    other_ref,
    cells_ref,
    surface_ref,
    tables_ref,
    blocks_ref,
    keep_ref,
    send_ref,
):
    result = continued(core_ref[0], numbers_ref, own_ref, other_ref, cells_ref, tables_ref)
    put_blocks(result, blocks_ref)
    values = jnp.where(core_ref[1] == 1, surface_ref[...], result)
    spread_rows(core_ref[0], tables_ref, values, keep_ref, send_ref)


def end_kernel(
    core_ref, numbers_ref, own_ref, other_ref, cells_ref, tables_ref, blocks_ref
):
    result = continued(core_ref[0], numbers_ref, own_ref, other_ref, cells_ref, tables_ref)
    put_blocks(result, blocks_ref)


def image_kernel(add, first_ref, second_ref, *refs):
    image_ref = refs[-1]
    lags, rows, width = image_ref.shape
    half = width // 2
    half_lags = lags // 2
    pairs = first_ref.shape[0] // 2
    for side, field_ref in enumerate((first_ref, second_ref)):
        for lag in range(lags):
            offset = lag - half_lags
            total = None
            for pair in range(pairs):
                source = field_ref[pair, half_lags - offset : half_lags - offset + rows, :]
                receiver = field_ref[
                    pairs + pair, half_lags + offset : half_lags + offset + rows, :
                ]
                term = source * receiver
                term = term[:, :half] + term[:, half:]
                total = term if total is None else total + term
            columns = slice(side * half, (side + 1) * half)
            if add:
                total = total + refs[0][lag, :, columns]
            image_ref[lag, :, columns] = total


def call(kernel, outs, *args):
    smem = {0, 1} if kernel_numbers(args) else {0}
    specs = [
        pl.BlockSpec(memory_space=pltpu.SMEM if place in smem else pltpu.VMEM)
        for place in range(len(args))
    ]
    return pl.pallas_call(
        kernel,
        out_shape=[jax.ShapeDtypeStruct(shape, jnp.float32) for shape in outs],
        in_specs=specs,
        out_specs=[pl.BlockSpec(memory_space=pltpu.VMEM)] * len(outs),
        compiler_params=pltpu.CompilerParams(vmem_limit_bytes=50 << 20),
    )(*args)


def kernel_numbers(args):
    return args[1].ndim == 1


def call_image(add, first, second, previous, shape):
    args = (first, second) + ((previous,) if add else ())
    return pl.pallas_call(
        functools.partial(image_kernel, add),
        out_shape=jax.ShapeDtypeStruct(shape, jnp.float32),
        in_specs=[pl.BlockSpec(memory_space=pltpu.VMEM)] * len(args),
        out_specs=pl.BlockSpec(memory_space=pltpu.VMEM),
        compiler_params=pltpu.CompilerParams(vmem_limit_bytes=50 << 20),
    )(*args)


def chip_shards(
    fields, surface, held_freqs, surface_freqs, ref_slowness, weights, regions, region_slowness
):
    lat = lax.axis_size("lat")
    depth = lax.axis_size("depth")
    depth_index = lax.axis_index("depth")
    core = depth_index % 2
    block_index = lax.axis_index("lat")
    place = block_index % 2
    field = block_index // 2
    at_first = core == 0
    freq_count = held_freqs.shape[1]
    field_count = 2 * freq_count
    rows, width = (fields.shape[4], fields.shape[5])
    half = width // 2
    total_rows = rows * lat
    half_lags = LAGS // 2
    swap = [(d, d + 1 - 2 * (d % 2)) for d in range(depth)]
    tables = jnp.asarray(dft_tables(width))

    def halves(value):
        first, second = (value[..., :half], value[..., half:])
        return (jnp.where(at_first, first, second), jnp.where(at_first, second, first))

    def swapped(value):
        return lax.ppermute(value, "depth", swap)

    def sent(blocks):
        return lax.all_to_all(blocks, "lat", split_axis=0, concat_axis=0, tiled=True)

    def side_by_side(value):
        return jnp.concatenate([value[0], value[1]], axis=-1)

    flat = fields[0].reshape(2, field_count, rows, width)
    own, other = halves(flat)
    own, other = (side_by_side(own), swapped(side_by_side(other)))
    both = jnp.stack(
        [jnp.where(at_first, own, other), jnp.where(at_first, other, own)], axis=1
    ).reshape(lat, rows, width)
    held = sent(both).reshape(total_rows, width)

    region_ids = jnp.arange(REGIONS, dtype=jnp.int32)
    cell = jnp.zeros((rows, width), jnp.float32)
    for region in range(REGIONS):
        cell = jnp.where(regions[0, 0] == region, region_slowness[0, 0, region], cell)
    numbers = jnp.concatenate(
        [ref_slowness[0, 0], held_freqs[0].astype(jnp.float32) * omega_step]
    )
    other_numbers = swapped(numbers)
    after_first = [((d + 2) % depth, d) for d in range(0, depth, 2)]
    after_second = [((d + 2) % depth, d + 1) for d in range(0, depth, 2)]

    def fetched(for_first, for_second):
        return jnp.where(
            at_first,
            lax.ppermute(for_first, "depth", after_first),
            lax.ppermute(for_second, "depth", after_second),
        )

    next_numbers = fetched(numbers, numbers)
    section_numbers = (
        jnp.where(at_first, numbers, other_numbers),
        jnp.where(at_first, other_numbers, numbers),
        next_numbers,
    )
    first_numbers = jnp.where(place == 0, section_numbers[0], section_numbers[1])
    second_numbers = jnp.where(place == 0, section_numbers[1], section_numbers[2])
    takes_surface = (depth_index // 2 == depth // 2 - 1) & (place == 1)
    freq = field % freq_count
    freq_ids = jnp.arange(freq_count, dtype=jnp.int32)

    def picked(values):
        return jnp.sum(jnp.where(freq_ids == freq, values, 0.0))

    sign = jnp.where(field < freq_count, -1.0, 1.0)
    omega_one = picked(first_numbers[2:])
    omega_two = jnp.where(
        takes_surface, picked(surface_freqs.astype(jnp.float32) * omega_step), omega_one
    )
    numbers_one = jnp.stack([omega_one, sign, first_numbers[0], first_numbers[1]])
    numbers_two = jnp.stack([omega_two, sign, second_numbers[0], second_numbers[1]])
    core_pair = jnp.stack([core, takes_surface.astype(jnp.int32)])

    cells = jnp.stack([weights[0, 0], cell])
    own_cells, other_cells = halves(cells)
    other_cells = swapped(other_cells)
    third = fetched(cells[..., :half], cells[..., half:])
    zero = jnp.where(at_first, own_cells, other_cells)
    one = jnp.where(at_first, other_cells, own_cells)

    def cell_blocks(even, odd):
        pair = jnp.stack([even, odd])
        return jnp.broadcast_to(pair[None], (lat // 2,) + pair.shape).reshape(
            (lat,) + even.shape
        )

    cells_one = sent(cell_blocks(zero, one))
    cells_two = sent(cell_blocks(one, third))
    surface_half, _ = halves(surface.reshape(2, field_count, rows, width))
    surface_half = side_by_side(surface_half)
    surface_blocks = jnp.broadcast_to(
        surface_half[:, None], (field_count, 2, rows, width)
    ).reshape(lat, rows, width)
    above = sent(surface_blocks).reshape(total_rows, width)

    spread = [(total_rows // 2, width)] * 2
    shifted = [(2, total_rows // 2, width)] * 2
    blocks = (lat, rows + 2 * half_lags, width)
    middle = functools.partial(middle_kernel, 1.0 / (total_rows * width))
    image_shape = (LAGS, rows, width)

    keep, send = call(start_kernel, spread, core_pair, held, tables)
    keep, send = call(middle, shifted, core_pair, numbers_one, keep, swapped(send), tables)
    result, keep, send = call(
        turn_kernel,
        [blocks] + spread,
        core_pair,
        numbers_one,
        keep,
        swapped(send),
        cells_one,
        above,
        tables,
    )
    first_out = sent(result).reshape((field_count, 2) + blocks[1:])
    keep, send = call(middle, shifted, core_pair, numbers_two, keep, swapped(send), tables)
    (result,) = call(
        end_kernel, [blocks], core_pair, numbers_two, keep, swapped(send), cells_two, tables
    )
    second_out = sent(result).reshape((field_count, 2) + blocks[1:])

    mine = jnp.where(at_first, first_out[:, 0], first_out[:, 1])
    theirs = swapped(jnp.where(at_first, first_out[:, 1], first_out[:, 0]))
    image = call_image(
        False,
        jnp.where(at_first, mine, theirs),
        jnp.where(at_first, theirs, mine),
        None,
        image_shape,
    )
    below = lax.ppermute(
        jnp.where(at_first, second_out[:, 0], second_out[:, 1]),
        "depth",
        [(d, (d + 1) % depth) for d in range(depth)],
    )
    down = lax.ppermute(
        second_out[:, 1], "depth", [(d, (d + 2) % depth) for d in range(0, depth, 2)]
    )
    left = jnp.where(at_first, down, below)
    right = jnp.where(at_first, below, second_out[:, 0])
    image = call_image(True, left, right, image, image_shape)
    inner = slice(half_lags, half_lags + rows)
    fields_out = jnp.stack(
        [
            jnp.concatenate([left[:, inner, :half], right[:, inner, :half]], axis=-1),
            jnp.concatenate([left[:, inner, half:], right[:, inner, half:]], axis=-1),
        ]
    ).reshape(fields.shape)
    return (fields_out, image[None, None])


def solution(mesh):
    in_specs = (
        P("depth", None, None, None, "lat", None),
        P(None, None, None, "lat", None),
        P("depth", None),
        P(),
        P("depth", None, None),
        P("depth", None, "lat", None),
        P("depth", None, "lat", None),
        P("depth", None, None),
    )
    out_specs = (P("depth", None, None, None, "lat", None), P("depth", None, None, "lat", None))

    def body(*args):
        fields = args[0]
        one_to_a_chip = lax.axis_size("lat") == 2 * fields.shape[2] * fields.shape[3]
        square = fields.shape[4] * lax.axis_size("lat") == fields.shape[5]
        if one_to_a_chip and square and lax.axis_size("depth") % 2 == 0:
            return chip_shards(*args)
        return shards(*args)

    return jax.shard_map(body, mesh=mesh, in_specs=in_specs, out_specs=out_specs, check_vma=False)
```

```python
import functools
import math

import jax
import jax.numpy as jnp
import ml_dtypes
import numpy as np
from jax import lax
from jax.experimental import pallas as pl
from jax.experimental.pallas import tpu as pltpu
from jax.sharding import PartitionSpec as P

LAGS = 16
REGIONS = 8


omega_step = 0.04
depth_step = 1.0
exact_math = lax.Precision.HIGHEST


def with_halo(cells, sides, width):
    for axis, dim in sides:
        count = lax.axis_size(axis)
        ends = count - 1
        head = lax.slice_in_dim(cells, 0, width, axis=dim)
        tail = lax.slice_in_dim(cells, cells.shape[dim] - width, cells.shape[dim], axis=dim)
        cells = jnp.concatenate(
            [
                lax.ppermute(tail, axis, [(i, (i + 1) % count) for i in range(ends)]),
                cells,
                lax.ppermute(head, axis, [((i + 1) % count, i) for i in range(ends)]),
            ],
            axis=dim,
        )
    return cells


def passed_along(value, axis, steps):
    count = lax.axis_size(axis)
    leading, last = (max(0, -steps), min(count, count - steps))
    return lax.ppermute(value, axis, [(source, source + steps) for source in range(leading, last)])


def factor_pair(length):
    first_len = 1
    for divisor in range(1, math.isqrt(length) + 1):
        if length % divisor == 0:
            first_len = divisor
    return (first_len, length // first_len)


def unit_phase(product_index, period, direction):
    turning = direction * 2.0 * math.pi / period * product_index.astype(jnp.float32)
    return (jnp.cos(turning), jnp.sin(turning))


def transform_tables(first_len, second_len, direction):
    first_range = jnp.arange(first_len, dtype=jnp.int32)
    second_range = jnp.arange(second_len, dtype=jnp.int32)
    outer_table = unit_phase(
        first_range[:, None] * first_range[None, :] % first_len, first_len, direction
    )
    twist_table = unit_phase(
        first_range[:, None] * second_range[None, :] % (first_len * second_len),
        first_len * second_len,
        direction,
    )
    inner_table = unit_phase(
        second_range[:, None] * second_range[None, :] % second_len, second_len, direction
    )
    return (outer_table, twist_table, inner_table)


def complex_product(pattern, values, table_pair):
    real_times = jnp.einsum(pattern, values[0], table_pair[0], precision=exact_math)
    imag_times = jnp.einsum(pattern, values[1], table_pair[1], precision=exact_math)
    joint_times = jnp.einsum(
        pattern, values[0] + values[1], table_pair[0] + table_pair[1], precision=exact_math
    )
    return jnp.stack([real_times - imag_times, joint_times - real_times - imag_times])


def complex_scale(values, factor):
    return jnp.stack(
        [
            values[0] * factor[0] - values[1] * factor[1],
            values[0] * factor[1] + values[1] * factor[0],
        ]
    )


def wave_numbers(positions, length):
    folded = jnp.where(positions < length // 2, positions, positions - length)
    return folded.astype(jnp.float32) * (2.0 * math.pi / length)


def forward_rows(values, tables, lane_count):
    groups, row_count, col_count = (values.shape[1], values.shape[2], values.shape[3])
    outer_table, twist_table, inner_table = tables
    split_first = outer_table[0].shape[0]
    split_second = inner_table[0].shape[0]
    shaped = values.reshape(2, groups, row_count, split_first, split_second)
    segmented = complex_product("grjm,kj->gkmr", shaped, outer_table)
    segmented = complex_scale(segmented, (twist_table[0][:, :, None], twist_table[1][:, :, None]))
    segmented = complex_product("gkmr,lm->gklr", segmented, inner_table)
    return segmented.reshape(2, groups, lane_count, col_count * row_count // lane_count)


def forward_columns(values, tables, lane_count, col_block, row_count):
    groups = values.shape[1]
    outer_table, twist_table, inner_table = tables
    shaped = values.reshape(2, groups, lane_count, col_block, row_count)
    segmented = complex_product("gscr,ks->gkcr", shaped, outer_table)
    segmented = complex_scale(segmented, (twist_table[0][:, None, :], twist_table[1][:, None, :]))
    segmented = complex_product("gkcr,lr->gckl", segmented, inner_table)
    return segmented.reshape(2, groups, col_block, lane_count * row_count)


def inverse_columns(values, tables, lane_count, row_count):
    groups, col_block = (values.shape[1], values.shape[2])
    outer_table, twist_table, inner_table = tables
    shaped = values.reshape(2, groups, col_block, lane_count, row_count)
    segmented = complex_product("gckl,lr->gckr", shaped, inner_table)
    segmented = complex_scale(segmented, twist_table)
    segmented = complex_product("gckr,ks->gscr", segmented, outer_table)
    return segmented.reshape(2, groups, lane_count, col_block * row_count)


def inverse_rows(values, tables, depth_rows):
    groups = values.shape[1]
    outer_table, twist_table, inner_table = tables
    split_first = outer_table[0].shape[0]
    split_second = inner_table[0].shape[0]
    shaped = values.reshape(2, groups, split_first, split_second, depth_rows)
    segmented = complex_product("gklr,lm->gkmr", shaped, inner_table)
    segmented = complex_scale(segmented, (twist_table[0][:, :, None], twist_table[1][:, :, None]))
    segmented = complex_product("gkmr,kj->grjm", segmented, outer_table)
    return segmented.reshape(2, groups, depth_rows, split_first * split_second)


def level_step(
    wave_state, omega_batch, slow_pair, weight_rows, cell_rows, squared, tables_y, tables_x, layout
):
    lane_count, row_count, col_block, margin = layout
    freq_count = wave_state.shape[2]
    col_count = wave_state.shape[4]
    sign_pair = jnp.array([-1.0, 1.0], jnp.float32)
    flat_state = wave_state.reshape(2, 2 * freq_count, row_count, col_count)
    spectra = forward_rows(flat_state, tables_y[0], lane_count)
    spectra = lax.all_to_all(spectra, "lat", split_axis=2, concat_axis=2, tiled=True)
    spectra = forward_columns(spectra, tables_x[0], lane_count, col_block, row_count)
    spectra = spectra.reshape(2, 2, freq_count, col_block, lane_count * row_count)
    wave_base = omega_batch[None, :, None, None] * slow_pair[:, None, None, None]
    wave_gap = wave_base * wave_base - squared[None, None]
    amplitude = jnp.exp(-jnp.sqrt(jnp.maximum(-wave_gap, 0.0)) * depth_step)
    turning = (
        sign_pair[None, :, None, None, None]
        * jnp.sqrt(jnp.maximum(wave_gap, 0.0))[:, None]
        * depth_step
    )
    factor = (amplitude[:, None] * jnp.cos(turning), amplitude[:, None] * jnp.sin(turning))
    shifted = complex_scale(spectra[:, None], factor)
    shifted = shifted.reshape(2, 4 * freq_count, col_block, lane_count * row_count)
    returned = inverse_columns(shifted, tables_x[1], lane_count, row_count)
    returned = lax.all_to_all(returned, "lat", split_axis=2, concat_axis=2, tiled=True)
    depth_rows = row_count + 2 * margin
    ref_fields = inverse_rows(returned, tables_y[1], depth_rows)
    ref_fields = ref_fields.reshape(2, 2, 2, freq_count, depth_rows, col_count) * (
        1.0 / (lane_count * row_count * col_count)
    )
    mixed_field = weight_rows * ref_fields[:, 0] + (1.0 - weight_rows) * ref_fields[:, 1]
    blend_slow = weight_rows * slow_pair[0] + (1.0 - weight_rows) * slow_pair[1]
    lens_angle = (
        sign_pair[:, None, None, None]
        * omega_batch[None, :, None, None]
        * (cell_rows - blend_slow)[None, None]
        * depth_step
    )
    return complex_scale(mixed_field, (jnp.cos(lens_angle), jnp.sin(lens_angle)))


def lag_products(padded, half_lags, row_count):
    lag_terms = []
    for lag_index in range(2 * half_lags):
        offset = lag_index - half_lags
        source_rows = padded[:, 0, :, half_lags - offset : half_lags - offset + row_count]
        receiver_rows = padded[:, 1, :, half_lags + offset : half_lags + offset + row_count]
        lag_terms.append(jnp.sum(source_rows * receiver_rows, axis=(0, 1)))
    return jnp.stack(lag_terms)


def shards(
    fields, surface, held_freqs, surface_freqs, ref_slowness, weights, regions, region_slowness
):
    lane_count = lax.axis_size("lat")
    row_count = fields.shape[4]
    col_count = fields.shape[5]
    col_block = col_count // lane_count
    total_rows = lane_count * row_count
    half_lags = LAGS // 2
    split_first, split_second = factor_pair(col_count)
    tables_y = (
        transform_tables(split_first, split_second, -1.0),
        transform_tables(split_first, split_second, 1.0),
    )
    tables_x = (
        transform_tables(lane_count, row_count, -1.0),
        transform_tables(lane_count, row_count, 1.0),
    )
    block_index = lax.axis_index("lat")
    storage_y = block_index * col_block + jnp.arange(col_block, dtype=jnp.int32)
    index_y = storage_y // split_second + split_first * (storage_y % split_second)
    storage_x = jnp.arange(total_rows, dtype=jnp.int32)
    index_x = storage_x // row_count + lane_count * (storage_x % row_count)
    squared = (
        wave_numbers(index_y, col_count)[:, None] ** 2
        + wave_numbers(index_x, total_rows)[None, :] ** 2
    )
    region_ids = jnp.arange(REGIONS, dtype=jnp.int32)
    matches = (regions[0][None] == region_ids[:, None, None, None]).astype(jnp.float32)
    cell_slowness = jnp.sum(matches * jnp.transpose(region_slowness[0])[:, :, None, None], axis=0)
    margin = 0
    weight_rows_all = weights[0]
    layout = (lane_count, row_count, col_block, margin)
    wave_state = fields[0]
    omega_batch = held_freqs[0].astype(jnp.float32) * omega_step
    images = [jnp.zeros((LAGS, row_count, col_count), jnp.float32)]
    for tick_index in range(2):
        result = level_step(
            wave_state,
            omega_batch,
            ref_slowness[0, 0],
            weight_rows_all[0],
            cell_slowness[0],
            squared,
            tables_y,
            tables_x,
            layout,
        )
        wave_state = result
        padded = with_halo(result, (("lat", 3),), half_lags)
        images[0] = images[0] + lag_products(padded, half_lags, row_count)
        if tick_index == 0:
            moved, moved_omega = passed_along((wave_state, omega_batch), "depth", 1)
            at_top = lax.axis_index("depth") == 0
            wave_state = jnp.where(at_top, surface, moved)
            omega_batch = jnp.where(
                at_top, surface_freqs.astype(jnp.float32) * omega_step, moved_omega
            )
    return (wave_state[None], jnp.stack(images)[None])

def split_halves(value):
    high = value.astype(jnp.bfloat16)
    low = (value - high.astype(jnp.float32)).astype(jnp.bfloat16)
    return (high, low)


def dft_tables(length):
    index = np.arange(length)
    turning = 2.0 * np.pi / length * (index[:, None] * index[None, :] % length)
    tables = []
    for exact in (np.cos(turning), np.sin(turning)):
        high = exact.astype(ml_dtypes.bfloat16)
        low = (exact - high.astype(np.float64)).astype(ml_dtypes.bfloat16)
        tables += [high, low]
    return np.stack(tables)


def dot(left, right):
    return jnp.dot(left, right, preferred_element_type=jnp.float32)


def three_pass_left(tables, which, high, low):
    table_high, table_low = (tables[2 * which], tables[2 * which + 1])
    return dot(table_high, high) + (dot(table_high, low) + dot(table_low, high))


def three_pass_right(tables, which, high, low):
    table_high, table_low = (tables[2 * which], tables[2 * which + 1])
    return dot(high, table_high) + (dot(low, table_high) + dot(high, table_low))


def dft_left(tables, values, direction):
    half = values.shape[1] // 2
    high, low = split_halves(values)
    even = three_pass_left(tables, 0, high, low)
    odd = three_pass_left(tables, 1, high, low)
    return (
        even[:, :half] - direction * odd[:, half:],
        even[:, half:] + direction * odd[:, :half],
    )


def dft_right(tables, values, direction):
    half = values.shape[0] // 2
    high, low = split_halves(values)
    even = three_pass_right(tables, 0, high, low)
    odd = three_pass_right(tables, 1, high, low)
    return (
        even[:half] - direction * odd[half:],
        even[half:] + direction * odd[:half],
    )


def spread_rows(core, tables, values, keep_ref, send_ref):
    half = values.shape[0] // 2
    real, imag = dft_left(tables, values, -1.0)
    both = jnp.concatenate([real, imag], axis=1)
    first, second = (both[:half], both[half:])
    at_first = core == 0
    keep_ref[...] = jnp.where(at_first, first, second)
    send_ref[...] = jnp.where(at_first, second, first)


def start_kernel(core_ref, blocks_ref, tables_ref, keep_ref, send_ref):
    rows = 2 * keep_ref.shape[0] // blocks_ref.shape[0]
    values = blocks_ref[:, :rows].reshape(2 * keep_ref.shape[0], blocks_ref.shape[2])
    spread_rows(core_ref[0], tables_ref, values, keep_ref, send_ref)


def folded(positions, length):
    moved = jnp.where(positions < length // 2, positions, positions - length)
    return moved.astype(jnp.float32) * (2.0 * math.pi / length)


def middle_kernel(scale, core_ref, numbers_ref, own_ref, other_ref, tables_ref, keep_ref, send_ref):
    core = core_ref[0]
    at_first = core == 0
    rows, width = own_ref.shape
    half = width // 2
    own, other = (own_ref[...], other_ref[...])
    first = jnp.where(at_first, own, other)
    second = jnp.where(at_first, other, own)
    values = jnp.concatenate(
        [
            jnp.concatenate([first[:, :half], second[:, :half]], axis=1),
            jnp.concatenate([first[:, half:], second[:, half:]], axis=1),
        ],
        axis=0,
    )
    real, imag = dft_right(tables_ref, values, -1.0)
    kx = folded(lax.broadcasted_iota(jnp.int32, (rows, 1), 0) + core * rows, 2 * rows)
    ky = folded(lax.broadcasted_iota(jnp.int32, (1, width), 1), width)
    squared = kx * kx + ky * ky
    omega, sign = (numbers_ref[0], numbers_ref[1])
    for ref_index in range(2):
        base = omega * numbers_ref[2 + ref_index]
        gap = base * base - squared
        amplitude = jnp.exp(-jnp.sqrt(jnp.maximum(-gap, 0.0))) * scale
        turning = jnp.sqrt(jnp.maximum(gap, 0.0))
        cosine = amplitude * jnp.cos(turning)
        sine = amplitude * (sign * jnp.sin(turning))
        shifted = jnp.concatenate([real * cosine - imag * sine, real * sine + imag * cosine], axis=0)
        back_real, back_imag = dft_right(tables_ref, shifted, 1.0)
        first = jnp.concatenate([back_real[:, :half], back_imag[:, :half]], axis=1)
        second = jnp.concatenate([back_real[:, half:], back_imag[:, half:]], axis=1)
        keep_ref[ref_index] = jnp.where(at_first, first, second)
        send_ref[ref_index] = jnp.where(at_first, second, first)


def continued(core, numbers_ref, own_ref, other_ref, cells_ref, tables_ref):
    at_first = core == 0
    rows, width = own_ref.shape[1:]
    half = width // 2
    fields = []
    for ref_index in range(2):
        own, other = (own_ref[ref_index], other_ref[ref_index])
        values = jnp.concatenate(
            [jnp.where(at_first, own, other), jnp.where(at_first, other, own)], axis=0
        )
        fields.append(dft_left(tables_ref, values, 1.0))
    weight = cells_ref[:, 0].reshape(2 * rows, half)
    cell = cells_ref[:, 1].reshape(2 * rows, half)
    rest = 1.0 - weight
    real = weight * fields[0][0] + rest * fields[1][0]
    imag = weight * fields[0][1] + rest * fields[1][1]
    blend = weight * numbers_ref[2] + rest * numbers_ref[3]
    angle = numbers_ref[1] * numbers_ref[0] * (cell - blend)
    cosine, sine = (jnp.cos(angle), jnp.sin(angle))
    return jnp.concatenate([real * cosine - imag * sine, real * sine + imag * cosine], axis=1)


def put_blocks(values, blocks_ref):
    count, tall, width = blocks_ref.shape
    rows = values.shape[0] // count
    margin = (tall - rows) // 2
    edge = jnp.zeros((margin, width), jnp.float32)
    for block in range(count):
        start = block * rows
        blocks_ref[block, margin : margin + rows] = values[start : start + rows]
        blocks_ref[block, :margin] = values[start - margin : start] if block else edge
        after = start + rows
        blocks_ref[block, margin + rows :] = (
            values[after : after + margin] if block < count - 1 else edge
        )


def turn_kernel(
    core_ref,
    numbers_ref,
    own_ref,
    other_ref,
    cells_ref,
    *refs,
):
    *piece_refs, tables_ref, blocks_ref, keep_ref, send_ref = refs
    result = continued(core_ref[0], numbers_ref, own_ref, other_ref, cells_ref, tables_ref)
    put_blocks(result, blocks_ref)
    above = jnp.concatenate([piece_ref[...] for piece_ref in piece_refs], axis=1)
    values = jnp.where(core_ref[1] == 1, above.reshape(result.shape), result)
    spread_rows(core_ref[0], tables_ref, values, keep_ref, send_ref)


def end_kernel(
    core_ref, numbers_ref, own_ref, other_ref, cells_ref, tables_ref, blocks_ref
):
    result = continued(core_ref[0], numbers_ref, own_ref, other_ref, cells_ref, tables_ref)
    put_blocks(result, blocks_ref)


def image_kernel(add, first_ref, second_ref, *refs):
    image_ref = refs[-1]
    lags, rows, width = image_ref.shape
    half = width // 2
    half_lags = lags // 2
    pairs = first_ref.shape[0] // 2
    for side, field_ref in enumerate((first_ref, second_ref)):
        for lag in range(lags):
            offset = lag - half_lags
            total = None
            for pair in range(pairs):
                source = field_ref[pair, half_lags - offset : half_lags - offset + rows, :]
                receiver = field_ref[
                    pairs + pair, half_lags + offset : half_lags + offset + rows, :
                ]
                term = source * receiver
                term = term[:, :half] + term[:, half:]
                total = term if total is None else total + term
            columns = slice(side * half, (side + 1) * half)
            if add:
                total = total + refs[0][lag, :, columns]
            image_ref[lag, :, columns] = total


def call(kernel, outs, *args):
    smem = {0, 1} if kernel_numbers(args) else {0}
    specs = [
        pl.BlockSpec(memory_space=pltpu.SMEM if place in smem else pltpu.VMEM)
        for place in range(len(args))
    ]
    return pl.pallas_call(
        kernel,
        out_shape=[jax.ShapeDtypeStruct(shape, jnp.float32) for shape in outs],
        in_specs=specs,
        out_specs=[pl.BlockSpec(memory_space=pltpu.VMEM)] * len(outs),
        compiler_params=pltpu.CompilerParams(vmem_limit_bytes=50 << 20),
        cost_estimate=pl.CostEstimate(
            flops=24 * math.prod(outs[-1]) * args[-1].shape[-1],
            bytes_accessed=4 * sum(math.prod(shape) for shape in outs),
            transcendentals=math.prod(outs[-1]),
        ),
    )(*args)


def kernel_numbers(args):
    return args[1].ndim == 1


def call_image(add, first, second, previous, shape):
    args = (first, second) + ((previous,) if add else ())
    return pl.pallas_call(
        functools.partial(image_kernel, add),
        out_shape=jax.ShapeDtypeStruct(shape, jnp.float32),
        in_specs=[pl.BlockSpec(memory_space=pltpu.VMEM)] * len(args),
        out_specs=pl.BlockSpec(memory_space=pltpu.VMEM),
        compiler_params=pltpu.CompilerParams(vmem_limit_bytes=50 << 20),
    )(*args)


def chip_shards(
    fields, surface, held_freqs, surface_freqs, ref_slowness, weights, regions, region_slowness
):
    lat = lax.axis_size("lat")
    depth = lax.axis_size("depth")
    depth_index = lax.axis_index("depth")
    core = depth_index % 2
    block_index = lax.axis_index("lat")
    place = block_index % 2
    field = block_index // 2
    at_first = core == 0
    freq_count = held_freqs.shape[1]
    field_count = 2 * freq_count
    rows, width = (fields.shape[4], fields.shape[5])
    half = width // 2
    total_rows = rows * lat
    half_lags = LAGS // 2
    swap = [(d, d + 1 - 2 * (d % 2)) for d in range(depth)]
    tables = jnp.asarray(dft_tables(width))

    def halves(value):
        first, second = (value[..., :half], value[..., half:])
        return (jnp.where(at_first, first, second), jnp.where(at_first, second, first))

    def swapped(value):
        return lax.ppermute(value, "depth", swap)

    def sent(blocks):
        return lax.all_to_all(blocks, "lat", split_axis=0, concat_axis=0, tiled=True)

    def side_by_side(value):
        return jnp.concatenate([value[0], value[1]], axis=-1)

    flat = fields[0].reshape(2, field_count, rows, width)
    own, other = halves(flat)
    own, other = (side_by_side(own), swapped(side_by_side(other)))
    both = jnp.stack(
        [jnp.where(at_first, own, other), jnp.where(at_first, other, own)], axis=1
    ).reshape(lat, rows, width)
    surface_half, _ = halves(surface.reshape(2, field_count, rows, width))
    surface_half = side_by_side(surface_half)
    part = rows // depth
    surface_part = lax.dynamic_slice_in_dim(
        surface_half, depth_index // 2 * (2 * part), 2 * part, axis=1
    ).reshape(lat, part, width)
    held = sent(jnp.concatenate([both, surface_part], axis=1))

    region_ids = jnp.arange(REGIONS, dtype=jnp.int32)
    cell = jnp.zeros((rows, width), jnp.float32)
    for region in range(REGIONS):
        cell = jnp.where(regions[0, 0] == region, region_slowness[0, 0, region], cell)
    numbers = jnp.concatenate(
        [ref_slowness[0, 0], held_freqs[0].astype(jnp.float32) * omega_step]
    )
    other_numbers = swapped(numbers)
    section_numbers = (
        jnp.where(at_first, numbers, other_numbers),
        jnp.where(at_first, other_numbers, numbers),
    )
    first_numbers = jnp.where(place == 0, section_numbers[0], section_numbers[1])
    below_chip = [
        (d * lat + j, (d * lat + j - 1) if j % 2 else ((d - 2) % depth * lat + j + 1))
        for d in range(depth)
        for j in range(lat)
    ]
    second_numbers = lax.ppermute(first_numbers, ("depth", "lat"), below_chip)
    takes_surface = (depth_index // 2 == depth // 2 - 1) & (place == 1)
    freq = field % freq_count
    freq_ids = jnp.arange(freq_count, dtype=jnp.int32)

    def picked(values):
        return jnp.sum(jnp.where(freq_ids == freq, values, 0.0))

    sign = jnp.where(field < freq_count, -1.0, 1.0)
    omega_one = picked(first_numbers[2:])
    omega_two = jnp.where(
        takes_surface, picked(surface_freqs.astype(jnp.float32) * omega_step), omega_one
    )
    numbers_one = jnp.stack([omega_one, sign, first_numbers[0], first_numbers[1]])
    numbers_two = jnp.stack([omega_two, sign, second_numbers[0], second_numbers[1]])
    core_pair = jnp.stack([core, takes_surface.astype(jnp.int32)])

    cells = jnp.stack([weights[0, 0], cell])
    own_cells, other_cells = halves(cells)
    other_cells = swapped(other_cells)
    zero = jnp.where(at_first, own_cells, other_cells)
    one = jnp.where(at_first, other_cells, own_cells)

    def cell_blocks(even, odd):
        pair = jnp.stack([even, odd])
        return jnp.broadcast_to(pair[None], (lat // 2,) + pair.shape).reshape(
            (lat,) + even.shape
        )

    blocks_one, held = lax.optimization_barrier((cell_blocks(zero, one), held))
    cells_one = sent(blocks_one)
    cells_two = lax.ppermute(cells_one, ("depth", "lat"), below_chip)

    last = depth // 2 - 1
    surface_part = held[:, rows:]
    pieces = []
    for piece in range(depth):
        plane, side = (piece // 2, piece % 2)
        if (plane, side) == (last, 1):
            pieces.append(surface_part)
            continue
        route = [
            ((2 * plane + c) * lat + 2 * f + side, (2 * last + c) * lat + 2 * f + 1)
            for c in range(2)
            for f in range(field_count)
        ]
        pieces.append(lax.ppermute(surface_part, ("depth", "lat"), route))

    spread = [(total_rows // 2, width)] * 2
    shifted = [(2, total_rows // 2, width)] * 2
    blocks = (lat, rows + 2 * half_lags, width)
    middle = functools.partial(middle_kernel, 1.0 / (total_rows * width))
    image_shape = (LAGS, rows, width)

    keep, send = call(start_kernel, spread, core_pair, held, tables)
    keep, send = call(middle, shifted, core_pair, numbers_one, keep, swapped(send), tables)
    result, keep, send = call(
        turn_kernel,
        [blocks] + spread,
        core_pair,
        numbers_one,
        keep,
        swapped(send),
        cells_one,
        *pieces,
        tables,
    )
    first_out = sent(result).reshape((field_count, 2) + blocks[1:])
    keep, send = call(middle, shifted, core_pair, numbers_two, keep, swapped(send), tables)
    (result,) = call(
        end_kernel, [blocks], core_pair, numbers_two, keep, swapped(send), cells_two, tables
    )
    second_out = sent(result).reshape((field_count, 2) + blocks[1:])

    mine = jnp.where(at_first, first_out[:, 0], first_out[:, 1])
    theirs = swapped(jnp.where(at_first, first_out[:, 1], first_out[:, 0]))
    image = call_image(
        False,
        jnp.where(at_first, mine, theirs),
        jnp.where(at_first, theirs, mine),
        None,
        image_shape,
    )
    below = lax.ppermute(
        jnp.where(at_first, second_out[:, 0], second_out[:, 1]),
        "depth",
        [(d, (d + 1) % depth) for d in range(depth)],
    )
    down = lax.ppermute(
        second_out[:, 1], "depth", [(d, (d + 2) % depth) for d in range(0, depth, 2)]
    )
    left = jnp.where(at_first, down, below)
    right = jnp.where(at_first, below, second_out[:, 0])
    image = call_image(True, left, right, image, image_shape)
    inner = slice(half_lags, half_lags + rows)
    fields_out = jnp.stack(
        [
            jnp.concatenate([left[:, inner, :half], right[:, inner, :half]], axis=-1),
            jnp.concatenate([left[:, inner, half:], right[:, inner, half:]], axis=-1),
        ]
    ).reshape(fields.shape)
    return (fields_out, image[None, None])


def solution(mesh):
    in_specs = (
        P("depth", None, None, None, "lat", None),
        P(None, None, None, "lat", None),
        P("depth", None),
        P(),
        P("depth", None, None),
        P("depth", None, "lat", None),
        P("depth", None, "lat", None),
        P("depth", None, None),
    )
    out_specs = (P("depth", None, None, None, "lat", None), P("depth", None, None, "lat", None))

    def body(*args):
        fields = args[0]
        one_to_a_chip = lax.axis_size("lat") == 2 * fields.shape[2] * fields.shape[3]
        square = fields.shape[4] * lax.axis_size("lat") == fields.shape[5]
        depth = lax.axis_size("depth")
        if one_to_a_chip and square and depth % 2 == 0 and fields.shape[4] % (8 * depth) == 0:
            return chip_shards(*args)
        return shards(*args)

    return jax.shard_map(body, mesh=mesh, in_specs=in_specs, out_specs=out_specs, check_vma=False)
```

```python
import functools
import math

import jax
import jax.numpy as jnp
import ml_dtypes
import numpy as np
from jax import lax
from jax.experimental import pallas as pl
from jax.experimental.pallas import tpu as pltpu
from jax.sharding import PartitionSpec as P

LAGS = 16
REGIONS = 8


omega_step = 0.04
depth_step = 1.0
exact_math = lax.Precision.HIGHEST


def with_halo(cells, sides, width):
    for axis, dim in sides:
        count = lax.axis_size(axis)
        ends = count - 1
        head = lax.slice_in_dim(cells, 0, width, axis=dim)
        tail = lax.slice_in_dim(cells, cells.shape[dim] - width, cells.shape[dim], axis=dim)
        cells = jnp.concatenate(
            [
                lax.ppermute(tail, axis, [(i, (i + 1) % count) for i in range(ends)]),
                cells,
                lax.ppermute(head, axis, [((i + 1) % count, i) for i in range(ends)]),
            ],
            axis=dim,
        )
    return cells


def passed_along(value, axis, steps):
    count = lax.axis_size(axis)
    leading, last = (max(0, -steps), min(count, count - steps))
    return lax.ppermute(value, axis, [(source, source + steps) for source in range(leading, last)])


def factor_pair(length):
    first_len = 1
    for divisor in range(1, math.isqrt(length) + 1):
        if length % divisor == 0:
            first_len = divisor
    return (first_len, length // first_len)


def unit_phase(product_index, period, direction):
    turning = direction * 2.0 * math.pi / period * product_index.astype(jnp.float32)
    return (jnp.cos(turning), jnp.sin(turning))


def transform_tables(first_len, second_len, direction):
    first_range = jnp.arange(first_len, dtype=jnp.int32)
    second_range = jnp.arange(second_len, dtype=jnp.int32)
    outer_table = unit_phase(
        first_range[:, None] * first_range[None, :] % first_len, first_len, direction
    )
    twist_table = unit_phase(
        first_range[:, None] * second_range[None, :] % (first_len * second_len),
        first_len * second_len,
        direction,
    )
    inner_table = unit_phase(
        second_range[:, None] * second_range[None, :] % second_len, second_len, direction
    )
    return (outer_table, twist_table, inner_table)


def complex_product(pattern, values, table_pair):
    real_times = jnp.einsum(pattern, values[0], table_pair[0], precision=exact_math)
    imag_times = jnp.einsum(pattern, values[1], table_pair[1], precision=exact_math)
    joint_times = jnp.einsum(
        pattern, values[0] + values[1], table_pair[0] + table_pair[1], precision=exact_math
    )
    return jnp.stack([real_times - imag_times, joint_times - real_times - imag_times])


def complex_scale(values, factor):
    return jnp.stack(
        [
            values[0] * factor[0] - values[1] * factor[1],
            values[0] * factor[1] + values[1] * factor[0],
        ]
    )


def wave_numbers(positions, length):
    folded = jnp.where(positions < length // 2, positions, positions - length)
    return folded.astype(jnp.float32) * (2.0 * math.pi / length)


def forward_rows(values, tables, lane_count):
    groups, row_count, col_count = (values.shape[1], values.shape[2], values.shape[3])
    outer_table, twist_table, inner_table = tables
    split_first = outer_table[0].shape[0]
    split_second = inner_table[0].shape[0]
    shaped = values.reshape(2, groups, row_count, split_first, split_second)
    segmented = complex_product("grjm,kj->gkmr", shaped, outer_table)
    segmented = complex_scale(segmented, (twist_table[0][:, :, None], twist_table[1][:, :, None]))
    segmented = complex_product("gkmr,lm->gklr", segmented, inner_table)
    return segmented.reshape(2, groups, lane_count, col_count * row_count // lane_count)


def forward_columns(values, tables, lane_count, col_block, row_count):
    groups = values.shape[1]
    outer_table, twist_table, inner_table = tables
    shaped = values.reshape(2, groups, lane_count, col_block, row_count)
    segmented = complex_product("gscr,ks->gkcr", shaped, outer_table)
    segmented = complex_scale(segmented, (twist_table[0][:, None, :], twist_table[1][:, None, :]))
    segmented = complex_product("gkcr,lr->gckl", segmented, inner_table)
    return segmented.reshape(2, groups, col_block, lane_count * row_count)


def inverse_columns(values, tables, lane_count, row_count):
    groups, col_block = (values.shape[1], values.shape[2])
    outer_table, twist_table, inner_table = tables
    shaped = values.reshape(2, groups, col_block, lane_count, row_count)
    segmented = complex_product("gckl,lr->gckr", shaped, inner_table)
    segmented = complex_scale(segmented, twist_table)
    segmented = complex_product("gckr,ks->gscr", segmented, outer_table)
    return segmented.reshape(2, groups, lane_count, col_block * row_count)


def inverse_rows(values, tables, depth_rows):
    groups = values.shape[1]
    outer_table, twist_table, inner_table = tables
    split_first = outer_table[0].shape[0]
    split_second = inner_table[0].shape[0]
    shaped = values.reshape(2, groups, split_first, split_second, depth_rows)
    segmented = complex_product("gklr,lm->gkmr", shaped, inner_table)
    segmented = complex_scale(segmented, (twist_table[0][:, :, None], twist_table[1][:, :, None]))
    segmented = complex_product("gkmr,kj->grjm", segmented, outer_table)
    return segmented.reshape(2, groups, depth_rows, split_first * split_second)


def level_step(
    wave_state, omega_batch, slow_pair, weight_rows, cell_rows, squared, tables_y, tables_x, layout
):
    lane_count, row_count, col_block, margin = layout
    freq_count = wave_state.shape[2]
    col_count = wave_state.shape[4]
    sign_pair = jnp.array([-1.0, 1.0], jnp.float32)
    flat_state = wave_state.reshape(2, 2 * freq_count, row_count, col_count)
    spectra = forward_rows(flat_state, tables_y[0], lane_count)
    spectra = lax.all_to_all(spectra, "lat", split_axis=2, concat_axis=2, tiled=True)
    spectra = forward_columns(spectra, tables_x[0], lane_count, col_block, row_count)
    spectra = spectra.reshape(2, 2, freq_count, col_block, lane_count * row_count)
    wave_base = omega_batch[None, :, None, None] * slow_pair[:, None, None, None]
    wave_gap = wave_base * wave_base - squared[None, None]
    amplitude = jnp.exp(-jnp.sqrt(jnp.maximum(-wave_gap, 0.0)) * depth_step)
    turning = (
        sign_pair[None, :, None, None, None]
        * jnp.sqrt(jnp.maximum(wave_gap, 0.0))[:, None]
        * depth_step
    )
    factor = (amplitude[:, None] * jnp.cos(turning), amplitude[:, None] * jnp.sin(turning))
    shifted = complex_scale(spectra[:, None], factor)
    shifted = shifted.reshape(2, 4 * freq_count, col_block, lane_count * row_count)
    returned = inverse_columns(shifted, tables_x[1], lane_count, row_count)
    returned = lax.all_to_all(returned, "lat", split_axis=2, concat_axis=2, tiled=True)
    depth_rows = row_count + 2 * margin
    ref_fields = inverse_rows(returned, tables_y[1], depth_rows)
    ref_fields = ref_fields.reshape(2, 2, 2, freq_count, depth_rows, col_count) * (
        1.0 / (lane_count * row_count * col_count)
    )
    mixed_field = weight_rows * ref_fields[:, 0] + (1.0 - weight_rows) * ref_fields[:, 1]
    blend_slow = weight_rows * slow_pair[0] + (1.0 - weight_rows) * slow_pair[1]
    lens_angle = (
        sign_pair[:, None, None, None]
        * omega_batch[None, :, None, None]
        * (cell_rows - blend_slow)[None, None]
        * depth_step
    )
    return complex_scale(mixed_field, (jnp.cos(lens_angle), jnp.sin(lens_angle)))


def lag_products(padded, half_lags, row_count):
    lag_terms = []
    for lag_index in range(2 * half_lags):
        offset = lag_index - half_lags
        source_rows = padded[:, 0, :, half_lags - offset : half_lags - offset + row_count]
        receiver_rows = padded[:, 1, :, half_lags + offset : half_lags + offset + row_count]
        lag_terms.append(jnp.sum(source_rows * receiver_rows, axis=(0, 1)))
    return jnp.stack(lag_terms)


def shards(
    fields, surface, held_freqs, surface_freqs, ref_slowness, weights, regions, region_slowness
):
    lane_count = lax.axis_size("lat")
    row_count = fields.shape[4]
    col_count = fields.shape[5]
    col_block = col_count // lane_count
    total_rows = lane_count * row_count
    half_lags = LAGS // 2
    split_first, split_second = factor_pair(col_count)
    tables_y = (
        transform_tables(split_first, split_second, -1.0),
        transform_tables(split_first, split_second, 1.0),
    )
    tables_x = (
        transform_tables(lane_count, row_count, -1.0),
        transform_tables(lane_count, row_count, 1.0),
    )
    block_index = lax.axis_index("lat")
    storage_y = block_index * col_block + jnp.arange(col_block, dtype=jnp.int32)
    index_y = storage_y // split_second + split_first * (storage_y % split_second)
    storage_x = jnp.arange(total_rows, dtype=jnp.int32)
    index_x = storage_x // row_count + lane_count * (storage_x % row_count)
    squared = (
        wave_numbers(index_y, col_count)[:, None] ** 2
        + wave_numbers(index_x, total_rows)[None, :] ** 2
    )
    region_ids = jnp.arange(REGIONS, dtype=jnp.int32)
    matches = (regions[0][None] == region_ids[:, None, None, None]).astype(jnp.float32)
    cell_slowness = jnp.sum(matches * jnp.transpose(region_slowness[0])[:, :, None, None], axis=0)
    margin = 0
    weight_rows_all = weights[0]
    layout = (lane_count, row_count, col_block, margin)
    wave_state = fields[0]
    omega_batch = held_freqs[0].astype(jnp.float32) * omega_step
    images = [jnp.zeros((LAGS, row_count, col_count), jnp.float32)]
    for tick_index in range(2):
        result = level_step(
            wave_state,
            omega_batch,
            ref_slowness[0, 0],
            weight_rows_all[0],
            cell_slowness[0],
            squared,
            tables_y,
            tables_x,
            layout,
        )
        wave_state = result
        padded = with_halo(result, (("lat", 3),), half_lags)
        images[0] = images[0] + lag_products(padded, half_lags, row_count)
        if tick_index == 0:
            moved, moved_omega = passed_along((wave_state, omega_batch), "depth", 1)
            at_top = lax.axis_index("depth") == 0
            wave_state = jnp.where(at_top, surface, moved)
            omega_batch = jnp.where(
                at_top, surface_freqs.astype(jnp.float32) * omega_step, moved_omega
            )
    return (wave_state[None], jnp.stack(images)[None])


def split_halves(value):
    high = value.astype(jnp.bfloat16)
    low = (value - high.astype(jnp.float32)).astype(jnp.bfloat16)
    return (high, low)


def dft_tables(length):
    index = np.arange(length)
    turning = 2.0 * np.pi / length * (index[: length // 4, None] * index[None, :] % length)
    tables = []
    for exact in (np.cos(turning), np.sin(turning)):
        high = exact.astype(ml_dtypes.bfloat16)
        low = (exact - high.astype(np.float64)).astype(ml_dtypes.bfloat16)
        tables += [high, low]
    cosine, sine = (jnp.asarray(np.stack(tables[:2])), jnp.asarray(np.stack(tables[2:])))
    turns = jnp.arange(length, dtype=jnp.int32) % 4
    quarters = []
    for _ in range(4):
        quarters.append(jnp.stack([cosine, sine]))
        swap_them = turns % 2 == 1
        first = jnp.where(swap_them, sine, cosine)
        second = jnp.where(swap_them, cosine, sine)
        cosine = jnp.where((turns == 1) | (turns == 2), -first, first)
        sine = jnp.where(turns >= 2, -second, second)
    return jnp.concatenate(quarters, axis=2).reshape(4, length, length)


def dot(left, right):
    return jnp.dot(left, right, preferred_element_type=jnp.float32)


def three_pass_left(tables, which, high, low):
    table_high, table_low = (tables[2 * which], tables[2 * which + 1])
    return dot(table_high, high) + (dot(table_high, low) + dot(table_low, high))


def three_pass_right(tables, which, high, low):
    table_high, table_low = (tables[2 * which], tables[2 * which + 1])
    return dot(high, table_high) + (dot(low, table_high) + dot(high, table_low))


def dft_left(tables, values, direction):
    half = values.shape[1] // 2
    high, low = split_halves(values)
    even = three_pass_left(tables, 0, high, low)
    odd = three_pass_left(tables, 1, high, low)
    return (
        even[:, :half] - direction * odd[:, half:],
        even[:, half:] + direction * odd[:, :half],
    )


def dft_right(tables, values, direction):
    half = values.shape[0] // 2
    high, low = split_halves(values)
    even = three_pass_right(tables, 0, high, low)
    odd = three_pass_right(tables, 1, high, low)
    return (
        even[:half] - direction * odd[half:],
        even[half:] + direction * odd[:half],
    )


def spread_rows(core, tables, values, keep_ref, send_ref):
    half = values.shape[0] // 2
    real, imag = dft_left(tables, values, -1.0)
    both = jnp.concatenate([real, imag], axis=1)
    first, second = (both[:half], both[half:])
    at_first = core == 0
    keep_ref[...] = jnp.where(at_first, first, second)
    send_ref[...] = jnp.where(at_first, second, first)


def start_kernel(core_ref, blocks_ref, tables_ref, keep_ref, send_ref):
    rows = 2 * keep_ref.shape[0] // blocks_ref.shape[0]
    values = blocks_ref[:, :rows].reshape(2 * keep_ref.shape[0], blocks_ref.shape[2])
    spread_rows(core_ref[0], tables_ref, values, keep_ref, send_ref)


def folded(positions, length):
    moved = jnp.where(positions < length // 2, positions, positions - length)
    return moved.astype(jnp.float32) * (2.0 * math.pi / length)


def middle_kernel(
    scale,
    core_ref,
    numbers_ref,
    own_ref,
    other_ref,
    tables_ref,
    keep_ref,
    send_ref,
    real_ref,
    imag_ref,
):
    core = core_ref[0]
    at_first = core == 0
    rows, width = own_ref.shape
    half = width // 2
    own, other = (own_ref[...], other_ref[...])
    first = jnp.where(at_first, own, other)
    second = jnp.where(at_first, other, own)
    values = jnp.concatenate(
        [
            jnp.concatenate([first[:, :half], second[:, :half]], axis=1),
            jnp.concatenate([first[:, half:], second[:, half:]], axis=1),
        ],
        axis=0,
    )
    real_ref[...], imag_ref[...] = dft_right(tables_ref, values, -1.0)
    kx = folded(lax.broadcasted_iota(jnp.int32, (rows, 1), 0) + core * rows, 2 * rows)
    ky = folded(lax.broadcasted_iota(jnp.int32, (1, width), 1), width)
    squared = kx * kx + ky * ky
    omega, sign = (numbers_ref[0], numbers_ref[1])

    @pl.loop(0, 2)
    def _(ref_index):
        real, imag = (real_ref[...], imag_ref[...])
        base = omega * numbers_ref[2 + ref_index]
        gap = base * base - squared
        amplitude = jnp.exp(-jnp.sqrt(jnp.maximum(-gap, 0.0))) * scale
        turning = jnp.sqrt(jnp.maximum(gap, 0.0))
        cosine = amplitude * jnp.cos(turning)
        sine = amplitude * (sign * jnp.sin(turning))
        shifted = jnp.concatenate([real * cosine - imag * sine, real * sine + imag * cosine], axis=0)
        back_real, back_imag = dft_right(tables_ref, shifted, 1.0)
        first = jnp.concatenate([back_real[:, :half], back_imag[:, :half]], axis=1)
        second = jnp.concatenate([back_real[:, half:], back_imag[:, half:]], axis=1)
        keep_ref[ref_index] = jnp.where(at_first, first, second)
        send_ref[ref_index] = jnp.where(at_first, second, first)


def continued(core, numbers_ref, own_ref, other_ref, cells_ref, tables_ref, real_ref, imag_ref):
    at_first = core == 0
    rows, width = own_ref.shape[1:]
    half = width // 2

    @pl.loop(0, 2)
    def _(ref_index):
        own, other = (own_ref[ref_index], other_ref[ref_index])
        values = jnp.concatenate(
            [jnp.where(at_first, own, other), jnp.where(at_first, other, own)], axis=0
        )
        real_ref[ref_index], imag_ref[ref_index] = dft_left(tables_ref, values, 1.0)

    weight = cells_ref[:, 0].reshape(2 * rows, half)
    cell = cells_ref[:, 1].reshape(2 * rows, half)
    rest = 1.0 - weight
    real = weight * real_ref[0] + rest * real_ref[1]
    imag = weight * imag_ref[0] + rest * imag_ref[1]
    blend = weight * numbers_ref[2] + rest * numbers_ref[3]
    angle = numbers_ref[1] * numbers_ref[0] * (cell - blend)
    cosine, sine = (jnp.cos(angle), jnp.sin(angle))
    return jnp.concatenate([real * cosine - imag * sine, real * sine + imag * cosine], axis=1)


def put_blocks(values, blocks_ref):
    count, tall, width = blocks_ref.shape
    rows = values.shape[0] // count
    margin = (tall - rows) // 2
    edge = jnp.zeros((margin, width), jnp.float32)
    for block in range(count):
        start = block * rows
        blocks_ref[block, margin : margin + rows] = values[start : start + rows]
        blocks_ref[block, :margin] = values[start - margin : start] if block else edge
        after = start + rows
        blocks_ref[block, margin + rows :] = (
            values[after : after + margin] if block < count - 1 else edge
        )


def turn_kernel(
    core_ref,
    numbers_ref,
    own_ref,
    other_ref,
    cells_ref,
    *refs,
):
    *piece_refs, tables_ref, blocks_ref, keep_ref, send_ref, real_ref, imag_ref = refs
    result = continued(
        core_ref[0], numbers_ref, own_ref, other_ref, cells_ref, tables_ref, real_ref, imag_ref
    )
    put_blocks(result, blocks_ref)
    above = jnp.concatenate([piece_ref[...] for piece_ref in piece_refs], axis=1)
    values = jnp.where(core_ref[1] == 1, above.reshape(result.shape), result)
    spread_rows(core_ref[0], tables_ref, values, keep_ref, send_ref)


def end_kernel(
    core_ref,
    numbers_ref,
    own_ref,
    other_ref,
    cells_ref,
    tables_ref,
    blocks_ref,
    real_ref,
    imag_ref,
):
    result = continued(
        core_ref[0], numbers_ref, own_ref, other_ref, cells_ref, tables_ref, real_ref, imag_ref
    )
    put_blocks(result, blocks_ref)


def image_kernel(add, first_ref, second_ref, *refs):
    image_ref = refs[-1]
    lags, rows, width = image_ref.shape
    half = width // 2
    half_lags = lags // 2
    pairs = first_ref.shape[0] // 2
    for side, field_ref in enumerate((first_ref, second_ref)):
        for lag in range(lags):
            offset = lag - half_lags
            total = None
            for pair in range(pairs):
                source = field_ref[pair, half_lags - offset : half_lags - offset + rows, :]
                receiver = field_ref[
                    pairs + pair, half_lags + offset : half_lags + offset + rows, :
                ]
                term = source * receiver
                term = term[:, :half] + term[:, half:]
                total = term if total is None else total + term
            columns = slice(side * half, (side + 1) * half)
            if add:
                total = total + refs[0][lag, :, columns]
            image_ref[lag, :, columns] = total


def call(kernel, outs, scratch, *args):
    smem = {0, 1} if kernel_numbers(args) else {0}
    specs = [
        pl.BlockSpec(memory_space=pltpu.SMEM if place in smem else pltpu.VMEM)
        for place in range(len(args))
    ]
    return pl.pallas_call(
        kernel,
        out_shape=[jax.ShapeDtypeStruct(shape, jnp.float32) for shape in outs],
        in_specs=specs,
        out_specs=[pl.BlockSpec(memory_space=pltpu.VMEM)] * len(outs),
        scratch_shapes=[pltpu.VMEM(shape, jnp.float32) for shape in scratch],
        compiler_params=pltpu.CompilerParams(vmem_limit_bytes=50 << 20),
        cost_estimate=pl.CostEstimate(
            flops=24 * math.prod(outs[-1]) * args[-1].shape[-1],
            bytes_accessed=4 * sum(math.prod(shape) for shape in outs),
            transcendentals=math.prod(outs[-1]),
        ),
    )(*args)


def kernel_numbers(args):
    return args[1].ndim == 1


def call_image(add, first, second, previous, shape):
    args = (first, second) + ((previous,) if add else ())
    return pl.pallas_call(
        functools.partial(image_kernel, add),
        out_shape=jax.ShapeDtypeStruct(shape, jnp.float32),
        in_specs=[pl.BlockSpec(memory_space=pltpu.VMEM)] * len(args),
        out_specs=pl.BlockSpec(memory_space=pltpu.VMEM),
        compiler_params=pltpu.CompilerParams(vmem_limit_bytes=50 << 20),
    )(*args)


def chip_shards(
    fields, surface, held_freqs, surface_freqs, ref_slowness, weights, regions, region_slowness
):
    lat = lax.axis_size("lat")
    depth = lax.axis_size("depth")
    depth_index = lax.axis_index("depth")
    core = depth_index % 2
    block_index = lax.axis_index("lat")
    place = block_index % 2
    field = block_index // 2
    at_first = core == 0
    freq_count = held_freqs.shape[1]
    field_count = 2 * freq_count
    rows, width = (fields.shape[4], fields.shape[5])
    half = width // 2
    total_rows = rows * lat
    half_lags = LAGS // 2
    swap = [(d, d + 1 - 2 * (d % 2)) for d in range(depth)]
    tables = dft_tables(width)

    def halves(value):
        first, second = (value[..., :half], value[..., half:])
        return (jnp.where(at_first, first, second), jnp.where(at_first, second, first))

    def swapped(value):
        return lax.ppermute(value, "depth", swap)

    def sent(blocks):
        return lax.all_to_all(blocks, "lat", split_axis=0, concat_axis=0, tiled=True)

    def side_by_side(value):
        return jnp.concatenate([value[0], value[1]], axis=-1)

    flat = fields[0].reshape(2, field_count, rows, width)
    own, other = halves(flat)
    own, other = (side_by_side(own), swapped(side_by_side(other)))
    both = jnp.stack(
        [jnp.where(at_first, own, other), jnp.where(at_first, other, own)], axis=1
    ).reshape(lat, rows, width)
    surface_half, _ = halves(surface.reshape(2, field_count, rows, width))
    surface_half = side_by_side(surface_half)
    part = rows // depth
    surface_part = lax.dynamic_slice_in_dim(
        surface_half, depth_index // 2 * (2 * part), 2 * part, axis=1
    ).reshape(lat, part, width)
    held = sent(jnp.concatenate([both, surface_part], axis=1))

    region_ids = jnp.arange(REGIONS, dtype=jnp.int32)
    cell = jnp.zeros((rows, width), jnp.float32)
    for region in range(REGIONS):
        cell = jnp.where(regions[0, 0] == region, region_slowness[0, 0, region], cell)
    numbers = jnp.concatenate(
        [ref_slowness[0, 0], held_freqs[0].astype(jnp.float32) * omega_step]
    )
    other_numbers = swapped(numbers)
    section_numbers = (
        jnp.where(at_first, numbers, other_numbers),
        jnp.where(at_first, other_numbers, numbers),
    )
    first_numbers = jnp.where(place == 0, section_numbers[0], section_numbers[1])
    below_chip = [
        (d * lat + j, (d * lat + j - 1) if j % 2 else ((d - 2) % depth * lat + j + 1))
        for d in range(depth)
        for j in range(lat)
    ]
    second_numbers = lax.ppermute(first_numbers, ("depth", "lat"), below_chip)
    takes_surface = (depth_index // 2 == depth // 2 - 1) & (place == 1)
    freq = field % freq_count
    freq_ids = jnp.arange(freq_count, dtype=jnp.int32)

    def picked(values):
        return jnp.sum(jnp.where(freq_ids == freq, values, 0.0))

    sign = jnp.where(field < freq_count, -1.0, 1.0)
    omega_one = picked(first_numbers[2:])
    omega_two = jnp.where(
        takes_surface, picked(surface_freqs.astype(jnp.float32) * omega_step), omega_one
    )
    numbers_one = jnp.stack([omega_one, sign, first_numbers[0], first_numbers[1]])
    numbers_two = jnp.stack([omega_two, sign, second_numbers[0], second_numbers[1]])
    core_pair = jnp.stack([core, takes_surface.astype(jnp.int32)])

    cells = jnp.stack([weights[0, 0], cell])
    own_cells, other_cells = halves(cells)
    other_cells = swapped(other_cells)
    zero = jnp.where(at_first, own_cells, other_cells)
    one = jnp.where(at_first, other_cells, own_cells)

    def cell_blocks(even, odd):
        pair = jnp.stack([even, odd])
        return jnp.broadcast_to(pair[None], (lat // 2,) + pair.shape).reshape(
            (lat,) + even.shape
        )

    blocks_one, held, numbers_one, numbers_two = lax.optimization_barrier(
        (cell_blocks(zero, one), held, numbers_one, numbers_two)
    )
    cells_one = sent(blocks_one)
    cells_two = lax.ppermute(cells_one, ("depth", "lat"), below_chip)

    last = depth // 2 - 1
    surface_part = held[:, rows:]
    pieces = []
    for piece in range(depth):
        plane, side = (piece // 2, piece % 2)
        if (plane, side) == (last, 1):
            pieces.append(surface_part)
            continue
        route = [
            ((2 * plane + c) * lat + 2 * f + side, (2 * last + c) * lat + 2 * f + 1)
            for c in range(2)
            for f in range(field_count)
        ]
        pieces.append(lax.ppermute(surface_part, ("depth", "lat"), route))

    spread = [(total_rows // 2, width)] * 2
    shifted = [(2, total_rows // 2, width)] * 2
    blocks = (lat, rows + 2 * half_lags, width)
    middle = functools.partial(middle_kernel, 1.0 / (total_rows * width))
    image_shape = (LAGS, rows, width)

    spectrum = [(total_rows // 2, width)] * 2
    mixed = [(2, total_rows, half)] * 2
    keep, send = call(start_kernel, spread, [], core_pair, held, tables)
    keep, send = call(
        middle, shifted, spectrum, core_pair, numbers_one, keep, swapped(send), tables
    )
    send = swapped(send)
    result, keep, send = call(
        turn_kernel,
        [blocks] + spread,
        mixed,
        core_pair,
        numbers_one,
        keep,
        send,
        cells_one,
        *pieces,
        tables,
    )
    first_out = sent(result).reshape((field_count, 2) + blocks[1:])
    keep, send = call(
        middle, shifted, spectrum, core_pair, numbers_two, keep, swapped(send), tables
    )
    (result,) = call(
        end_kernel,
        [blocks],
        mixed,
        core_pair,
        numbers_two,
        keep,
        swapped(send),
        cells_two,
        tables,
    )
    second_out = sent(result).reshape((field_count, 2) + blocks[1:])

    mine = jnp.where(at_first, first_out[:, 0], first_out[:, 1])
    theirs = swapped(jnp.where(at_first, first_out[:, 1], first_out[:, 0]))
    image = call_image(
        False,
        jnp.where(at_first, mine, theirs),
        jnp.where(at_first, theirs, mine),
        None,
        image_shape,
    )
    below = lax.ppermute(
        jnp.where(at_first, second_out[:, 0], second_out[:, 1]),
        "depth",
        [(d, (d + 1) % depth) for d in range(depth)],
    )
    down = lax.ppermute(
        second_out[:, 1], "depth", [(d, (d + 2) % depth) for d in range(0, depth, 2)]
    )
    left = jnp.where(at_first, down, below)
    right = jnp.where(at_first, below, second_out[:, 0])
    image = call_image(True, left, right, image, image_shape)
    inner = slice(half_lags, half_lags + rows)
    fields_out = jnp.stack(
        [
            jnp.concatenate([left[:, inner, :half], right[:, inner, :half]], axis=-1),
            jnp.concatenate([left[:, inner, half:], right[:, inner, half:]], axis=-1),
        ]
    ).reshape(fields.shape)
    return (fields_out, image[None, None])


def solution(mesh):
    in_specs = (
        P("depth", None, None, None, "lat", None),
        P(None, None, None, "lat", None),
        P("depth", None),
        P(),
        P("depth", None, None),
        P("depth", None, "lat", None),
        P("depth", None, "lat", None),
        P("depth", None, None),
    )
    out_specs = (P("depth", None, None, None, "lat", None), P("depth", None, None, "lat", None))

    def body(*args):
        fields = args[0]
        one_to_a_chip = lax.axis_size("lat") == 2 * fields.shape[2] * fields.shape[3]
        square = fields.shape[4] * lax.axis_size("lat") == fields.shape[5]
        depth = lax.axis_size("depth")
        if one_to_a_chip and square and depth % 2 == 0 and fields.shape[4] % (8 * depth) == 0:
            return chip_shards(*args)
        return shards(*args)

    return jax.shard_map(body, mesh=mesh, in_specs=in_specs, out_specs=out_specs, check_vma=False)
```

```python
import functools
import math

import jax
import jax.numpy as jnp
import ml_dtypes
import numpy as np
from jax import lax
from jax.experimental import pallas as pl
from jax.experimental.pallas import tpu as pltpu
from jax.sharding import PartitionSpec as P

LAGS = 16
REGIONS = 8


omega_step = 0.04
depth_step = 1.0
exact_math = lax.Precision.HIGHEST


def with_halo(cells, sides, width):
    for axis, dim in sides:
        count = lax.axis_size(axis)
        ends = count - 1
        head = lax.slice_in_dim(cells, 0, width, axis=dim)
        tail = lax.slice_in_dim(cells, cells.shape[dim] - width, cells.shape[dim], axis=dim)
        cells = jnp.concatenate(
            [
                lax.ppermute(tail, axis, [(i, (i + 1) % count) for i in range(ends)]),
                cells,
                lax.ppermute(head, axis, [((i + 1) % count, i) for i in range(ends)]),
            ],
            axis=dim,
        )
    return cells


def passed_along(value, axis, steps):
    count = lax.axis_size(axis)
    leading, last = (max(0, -steps), min(count, count - steps))
    return lax.ppermute(value, axis, [(source, source + steps) for source in range(leading, last)])


def factor_pair(length):
    first_len = 1
    for divisor in range(1, math.isqrt(length) + 1):
        if length % divisor == 0:
            first_len = divisor
    return (first_len, length // first_len)


def unit_phase(product_index, period, direction):
    turning = direction * 2.0 * math.pi / period * product_index.astype(jnp.float32)
    return (jnp.cos(turning), jnp.sin(turning))


def transform_tables(first_len, second_len, direction):
    first_range = jnp.arange(first_len, dtype=jnp.int32)
    second_range = jnp.arange(second_len, dtype=jnp.int32)
    outer_table = unit_phase(
        first_range[:, None] * first_range[None, :] % first_len, first_len, direction
    )
    twist_table = unit_phase(
        first_range[:, None] * second_range[None, :] % (first_len * second_len),
        first_len * second_len,
        direction,
    )
    inner_table = unit_phase(
        second_range[:, None] * second_range[None, :] % second_len, second_len, direction
    )
    return (outer_table, twist_table, inner_table)


def complex_product(pattern, values, table_pair):
    real_times = jnp.einsum(pattern, values[0], table_pair[0], precision=exact_math)
    imag_times = jnp.einsum(pattern, values[1], table_pair[1], precision=exact_math)
    joint_times = jnp.einsum(
        pattern, values[0] + values[1], table_pair[0] + table_pair[1], precision=exact_math
    )
    return jnp.stack([real_times - imag_times, joint_times - real_times - imag_times])


def complex_scale(values, factor):
    return jnp.stack(
        [
            values[0] * factor[0] - values[1] * factor[1],
            values[0] * factor[1] + values[1] * factor[0],
        ]
    )


def wave_numbers(positions, length):
    folded = jnp.where(positions < length // 2, positions, positions - length)
    return folded.astype(jnp.float32) * (2.0 * math.pi / length)


def forward_rows(values, tables, lane_count):
    groups, row_count, col_count = (values.shape[1], values.shape[2], values.shape[3])
    outer_table, twist_table, inner_table = tables
    split_first = outer_table[0].shape[0]
    split_second = inner_table[0].shape[0]
    shaped = values.reshape(2, groups, row_count, split_first, split_second)
    segmented = complex_product("grjm,kj->gkmr", shaped, outer_table)
    segmented = complex_scale(segmented, (twist_table[0][:, :, None], twist_table[1][:, :, None]))
    segmented = complex_product("gkmr,lm->gklr", segmented, inner_table)
    return segmented.reshape(2, groups, lane_count, col_count * row_count // lane_count)


def forward_columns(values, tables, lane_count, col_block, row_count):
    groups = values.shape[1]
    outer_table, twist_table, inner_table = tables
    shaped = values.reshape(2, groups, lane_count, col_block, row_count)
    segmented = complex_product("gscr,ks->gkcr", shaped, outer_table)
    segmented = complex_scale(segmented, (twist_table[0][:, None, :], twist_table[1][:, None, :]))
    segmented = complex_product("gkcr,lr->gckl", segmented, inner_table)
    return segmented.reshape(2, groups, col_block, lane_count * row_count)


def inverse_columns(values, tables, lane_count, row_count):
    groups, col_block = (values.shape[1], values.shape[2])
    outer_table, twist_table, inner_table = tables
    shaped = values.reshape(2, groups, col_block, lane_count, row_count)
    segmented = complex_product("gckl,lr->gckr", shaped, inner_table)
    segmented = complex_scale(segmented, twist_table)
    segmented = complex_product("gckr,ks->gscr", segmented, outer_table)
    return segmented.reshape(2, groups, lane_count, col_block * row_count)


def inverse_rows(values, tables, depth_rows):
    groups = values.shape[1]
    outer_table, twist_table, inner_table = tables
    split_first = outer_table[0].shape[0]
    split_second = inner_table[0].shape[0]
    shaped = values.reshape(2, groups, split_first, split_second, depth_rows)
    segmented = complex_product("gklr,lm->gkmr", shaped, inner_table)
    segmented = complex_scale(segmented, (twist_table[0][:, :, None], twist_table[1][:, :, None]))
    segmented = complex_product("gkmr,kj->grjm", segmented, outer_table)
    return segmented.reshape(2, groups, depth_rows, split_first * split_second)


def level_step(
    wave_state, omega_batch, slow_pair, weight_rows, cell_rows, squared, tables_y, tables_x, layout
):
    lane_count, row_count, col_block, margin = layout
    freq_count = wave_state.shape[2]
    col_count = wave_state.shape[4]
    sign_pair = jnp.array([-1.0, 1.0], jnp.float32)
    flat_state = wave_state.reshape(2, 2 * freq_count, row_count, col_count)
    spectra = forward_rows(flat_state, tables_y[0], lane_count)
    spectra = lax.all_to_all(spectra, "lat", split_axis=2, concat_axis=2, tiled=True)
    spectra = forward_columns(spectra, tables_x[0], lane_count, col_block, row_count)
    spectra = spectra.reshape(2, 2, freq_count, col_block, lane_count * row_count)
    wave_base = omega_batch[None, :, None, None] * slow_pair[:, None, None, None]
    wave_gap = wave_base * wave_base - squared[None, None]
    amplitude = jnp.exp(-jnp.sqrt(jnp.maximum(-wave_gap, 0.0)) * depth_step)
    turning = (
        sign_pair[None, :, None, None, None]
        * jnp.sqrt(jnp.maximum(wave_gap, 0.0))[:, None]
        * depth_step
    )
    factor = (amplitude[:, None] * jnp.cos(turning), amplitude[:, None] * jnp.sin(turning))
    shifted = complex_scale(spectra[:, None], factor)
    shifted = shifted.reshape(2, 4 * freq_count, col_block, lane_count * row_count)
    returned = inverse_columns(shifted, tables_x[1], lane_count, row_count)
    returned = lax.all_to_all(returned, "lat", split_axis=2, concat_axis=2, tiled=True)
    depth_rows = row_count + 2 * margin
    ref_fields = inverse_rows(returned, tables_y[1], depth_rows)
    ref_fields = ref_fields.reshape(2, 2, 2, freq_count, depth_rows, col_count) * (
        1.0 / (lane_count * row_count * col_count)
    )
    mixed_field = weight_rows * ref_fields[:, 0] + (1.0 - weight_rows) * ref_fields[:, 1]
    blend_slow = weight_rows * slow_pair[0] + (1.0 - weight_rows) * slow_pair[1]
    lens_angle = (
        sign_pair[:, None, None, None]
        * omega_batch[None, :, None, None]
        * (cell_rows - blend_slow)[None, None]
        * depth_step
    )
    return complex_scale(mixed_field, (jnp.cos(lens_angle), jnp.sin(lens_angle)))


def lag_products(padded, half_lags, row_count):
    lag_terms = []
    for lag_index in range(2 * half_lags):
        offset = lag_index - half_lags
        source_rows = padded[:, 0, :, half_lags - offset : half_lags - offset + row_count]
        receiver_rows = padded[:, 1, :, half_lags + offset : half_lags + offset + row_count]
        lag_terms.append(jnp.sum(source_rows * receiver_rows, axis=(0, 1)))
    return jnp.stack(lag_terms)


def shards(
    fields, surface, held_freqs, surface_freqs, ref_slowness, weights, regions, region_slowness
):
    lane_count = lax.axis_size("lat")
    row_count = fields.shape[4]
    col_count = fields.shape[5]
    col_block = col_count // lane_count
    total_rows = lane_count * row_count
    half_lags = LAGS // 2
    split_first, split_second = factor_pair(col_count)
    tables_y = (
        transform_tables(split_first, split_second, -1.0),
        transform_tables(split_first, split_second, 1.0),
    )
    tables_x = (
        transform_tables(lane_count, row_count, -1.0),
        transform_tables(lane_count, row_count, 1.0),
    )
    block_index = lax.axis_index("lat")
    storage_y = block_index * col_block + jnp.arange(col_block, dtype=jnp.int32)
    index_y = storage_y // split_second + split_first * (storage_y % split_second)
    storage_x = jnp.arange(total_rows, dtype=jnp.int32)
    index_x = storage_x // row_count + lane_count * (storage_x % row_count)
    squared = (
        wave_numbers(index_y, col_count)[:, None] ** 2
        + wave_numbers(index_x, total_rows)[None, :] ** 2
    )
    region_ids = jnp.arange(REGIONS, dtype=jnp.int32)
    matches = (regions[0][None] == region_ids[:, None, None, None]).astype(jnp.float32)
    cell_slowness = jnp.sum(matches * jnp.transpose(region_slowness[0])[:, :, None, None], axis=0)
    margin = 0
    weight_rows_all = weights[0]
    layout = (lane_count, row_count, col_block, margin)
    wave_state = fields[0]
    omega_batch = held_freqs[0].astype(jnp.float32) * omega_step
    images = [jnp.zeros((LAGS, row_count, col_count), jnp.float32)]
    for tick_index in range(2):
        result = level_step(
            wave_state,
            omega_batch,
            ref_slowness[0, 0],
            weight_rows_all[0],
            cell_slowness[0],
            squared,
            tables_y,
            tables_x,
            layout,
        )
        wave_state = result
        padded = with_halo(result, (("lat", 3),), half_lags)
        images[0] = images[0] + lag_products(padded, half_lags, row_count)
        if tick_index == 0:
            moved, moved_omega = passed_along((wave_state, omega_batch), "depth", 1)
            at_top = lax.axis_index("depth") == 0
            wave_state = jnp.where(at_top, surface, moved)
            omega_batch = jnp.where(
                at_top, surface_freqs.astype(jnp.float32) * omega_step, moved_omega
            )
    return (wave_state[None], jnp.stack(images)[None])


def split_halves(value):
    high = value.astype(jnp.bfloat16)
    low = (value - high.astype(jnp.float32)).astype(jnp.bfloat16)
    return (high, low)


def dft_tables(length):
    index = np.arange(length)
    turning = 2.0 * np.pi / length * (index[: length // 4, None] * index[None, :] % length)
    tables = []
    for exact in (np.cos(turning), np.sin(turning)):
        high = exact.astype(ml_dtypes.bfloat16)
        low = (exact - high.astype(np.float64)).astype(ml_dtypes.bfloat16)
        tables += [high, low]
    cosine, sine = (jnp.asarray(np.stack(tables[:2])), jnp.asarray(np.stack(tables[2:])))
    turns = jnp.arange(length, dtype=jnp.int32) % 4
    quarters = []
    for _ in range(4):
        quarters.append(jnp.stack([cosine, sine]))
        swap_them = turns % 2 == 1
        first = jnp.where(swap_them, sine, cosine)
        second = jnp.where(swap_them, cosine, sine)
        cosine = jnp.where((turns == 1) | (turns == 2), -first, first)
        sine = jnp.where(turns >= 2, -second, second)
    return jnp.concatenate(quarters, axis=2).reshape(4, length, length)


def dot(left, right):
    return jnp.dot(left, right, preferred_element_type=jnp.float32)


def three_pass_left(tables, which, high, low):
    table_high, table_low = (tables[2 * which], tables[2 * which + 1])
    return dot(table_high, high) + (dot(table_high, low) + dot(table_low, high))


def three_pass_right(tables, which, high, low):
    table_high, table_low = (tables[2 * which], tables[2 * which + 1])
    return dot(high, table_high) + (dot(low, table_high) + dot(high, table_low))


def dft_left(tables, values, direction):
    half = values.shape[1] // 2
    high, low = split_halves(values)
    even = three_pass_left(tables, 0, high, low)
    odd = three_pass_left(tables, 1, high, low)
    return (
        even[:, :half] - direction * odd[:, half:],
        even[:, half:] + direction * odd[:, :half],
    )


def dft_right(tables, values, direction):
    half = values.shape[0] // 2
    high, low = split_halves(values)
    even = three_pass_right(tables, 0, high, low)
    odd = three_pass_right(tables, 1, high, low)
    return (
        even[:half] - direction * odd[half:],
        even[half:] + direction * odd[:half],
    )


def spread_rows(core, tables, values, keep_ref, send_ref):
    half = values.shape[0] // 2
    real, imag = dft_left(tables, values, -1.0)
    both = jnp.concatenate([real, imag], axis=1)
    first, second = (both[:half], both[half:])
    at_first = core == 0
    keep_ref[...] = jnp.where(at_first, first, second)
    send_ref[...] = jnp.where(at_first, second, first)


def start_kernel(core_ref, blocks_ref, tables_ref, keep_ref, send_ref):
    rows = 2 * keep_ref.shape[0] // blocks_ref.shape[0]
    values = blocks_ref[:, :rows].reshape(2 * keep_ref.shape[0], blocks_ref.shape[2])
    spread_rows(core_ref[0], tables_ref, values, keep_ref, send_ref)


def series(square, first):
    total = jnp.ones_like(square)
    for step in range(first + 14, first, -2):
        total = 1.0 - square * (total * (1.0 / (step * (step - 1))))
    return total


def cos_sin(angle):
    quarter = 0.5 * angle
    square = quarter * quarter
    sine = quarter * series(square, 1)
    cosine = series(square, 0)
    return (1.0 - 2.0 * (sine * sine), 2.0 * (sine * cosine))


def folded(positions, length):
    moved = jnp.where(positions < length // 2, positions, positions - length)
    return moved.astype(jnp.float32) * (2.0 * math.pi / length)


def middle_kernel(
    scale,
    core_ref,
    numbers_ref,
    own_ref,
    other_ref,
    tables_ref,
    keep_ref,
    send_ref,
    real_ref,
    imag_ref,
):
    core = core_ref[0]
    at_first = core == 0
    rows, width = own_ref.shape
    half = width // 2
    own, other = (own_ref[...], other_ref[...])
    first = jnp.where(at_first, own, other)
    second = jnp.where(at_first, other, own)
    values = jnp.concatenate(
        [
            jnp.concatenate([first[:, :half], second[:, :half]], axis=1),
            jnp.concatenate([first[:, half:], second[:, half:]], axis=1),
        ],
        axis=0,
    )
    real_ref[...], imag_ref[...] = dft_right(tables_ref, values, -1.0)
    kx = folded(lax.broadcasted_iota(jnp.int32, (rows, 1), 0) + core * rows, 2 * rows)
    ky = folded(lax.broadcasted_iota(jnp.int32, (1, width), 1), width)
    squared = kx * kx + ky * ky
    omega, sign = (numbers_ref[0], numbers_ref[1])

    @pl.loop(0, 2)
    def _(ref_index):
        real, imag = (real_ref[...], imag_ref[...])
        base = omega * numbers_ref[2 + ref_index]
        gap = base * base - squared
        amplitude = jnp.exp(-jnp.sqrt(jnp.maximum(-gap, 0.0))) * scale
        turning = jnp.sqrt(jnp.maximum(gap, 0.0))
        cosine, sine = cos_sin(turning)
        cosine = amplitude * cosine
        sine = amplitude * (sign * sine)
        shifted = jnp.concatenate([real * cosine - imag * sine, real * sine + imag * cosine], axis=0)
        back_real, back_imag = dft_right(tables_ref, shifted, 1.0)
        first = jnp.concatenate([back_real[:, :half], back_imag[:, :half]], axis=1)
        second = jnp.concatenate([back_real[:, half:], back_imag[:, half:]], axis=1)
        keep_ref[ref_index] = jnp.where(at_first, first, second)
        send_ref[ref_index] = jnp.where(at_first, second, first)


def continued(core, numbers_ref, own_ref, other_ref, cells_ref, tables_ref, real_ref, imag_ref):
    at_first = core == 0
    rows, width = own_ref.shape[1:]
    half = width // 2

    @pl.loop(0, 2)
    def _(ref_index):
        own, other = (own_ref[ref_index], other_ref[ref_index])
        values = jnp.concatenate(
            [jnp.where(at_first, own, other), jnp.where(at_first, other, own)], axis=0
        )
        real_ref[ref_index], imag_ref[ref_index] = dft_left(tables_ref, values, 1.0)

    weight = cells_ref[:, 0].reshape(2 * rows, half)
    cell = cells_ref[:, 1].reshape(2 * rows, half)
    rest = 1.0 - weight
    real = weight * real_ref[0] + rest * real_ref[1]
    imag = weight * imag_ref[0] + rest * imag_ref[1]
    blend = weight * numbers_ref[2] + rest * numbers_ref[3]
    angle = numbers_ref[1] * numbers_ref[0] * (cell - blend)
    cosine, sine = cos_sin(angle)
    return jnp.concatenate([real * cosine - imag * sine, real * sine + imag * cosine], axis=1)


def put_blocks(values, blocks_ref):
    count, tall, width = blocks_ref.shape
    rows = values.shape[0] // count
    margin = (tall - rows) // 2
    edge = jnp.zeros((margin, width), jnp.float32)
    for block in range(count):
        start = block * rows
        blocks_ref[block, margin : margin + rows] = values[start : start + rows]
        blocks_ref[block, :margin] = values[start - margin : start] if block else edge
        after = start + rows
        blocks_ref[block, margin + rows :] = (
            values[after : after + margin] if block < count - 1 else edge
        )


def turn_kernel(
    core_ref,
    numbers_ref,
    own_ref,
    other_ref,
    cells_ref,
    *refs,
):
    *piece_refs, tables_ref, blocks_ref, keep_ref, send_ref, real_ref, imag_ref = refs
    result = continued(
        core_ref[0], numbers_ref, own_ref, other_ref, cells_ref, tables_ref, real_ref, imag_ref
    )
    put_blocks(result, blocks_ref)
    above = jnp.concatenate([piece_ref[...] for piece_ref in piece_refs], axis=1)
    values = jnp.where(core_ref[1] == 1, above.reshape(result.shape), result)
    spread_rows(core_ref[0], tables_ref, values, keep_ref, send_ref)


def end_kernel(
    core_ref,
    numbers_ref,
    own_ref,
    other_ref,
    cells_ref,
    tables_ref,
    blocks_ref,
    real_ref,
    imag_ref,
):
    result = continued(
        core_ref[0], numbers_ref, own_ref, other_ref, cells_ref, tables_ref, real_ref, imag_ref
    )
    put_blocks(result, blocks_ref)


def image_kernel(add, first_ref, second_ref, *refs):
    image_ref = refs[-1]
    lags, rows, width = image_ref.shape
    half = width // 2
    half_lags = lags // 2
    pairs = first_ref.shape[0] // 2
    for side, field_ref in enumerate((first_ref, second_ref)):
        for lag in range(lags):
            offset = lag - half_lags
            total = None
            for pair in range(pairs):
                source = field_ref[pair, half_lags - offset : half_lags - offset + rows, :]
                receiver = field_ref[
                    pairs + pair, half_lags + offset : half_lags + offset + rows, :
                ]
                term = source * receiver
                term = term[:, :half] + term[:, half:]
                total = term if total is None else total + term
            columns = slice(side * half, (side + 1) * half)
            if add:
                total = total + refs[0][lag, :, columns]
            image_ref[lag, :, columns] = total


def call(kernel, outs, scratch, *args):
    smem = {0, 1} if kernel_numbers(args) else {0}
    specs = [
        pl.BlockSpec(memory_space=pltpu.SMEM if place in smem else pltpu.VMEM)
        for place in range(len(args))
    ]
    return pl.pallas_call(
        kernel,
        out_shape=[jax.ShapeDtypeStruct(shape, jnp.float32) for shape in outs],
        in_specs=specs,
        out_specs=[pl.BlockSpec(memory_space=pltpu.VMEM)] * len(outs),
        scratch_shapes=[pltpu.VMEM(shape, jnp.float32) for shape in scratch],
        compiler_params=pltpu.CompilerParams(vmem_limit_bytes=50 << 20),
        cost_estimate=pl.CostEstimate(
            flops=24 * math.prod(outs[-1]) * args[-1].shape[-1],
            bytes_accessed=4 * sum(math.prod(shape) for shape in outs),
            transcendentals=math.prod(outs[-1]),
        ),
    )(*args)


def kernel_numbers(args):
    return args[1].ndim == 1


def call_image(add, first, second, previous, shape):
    args = (first, second) + ((previous,) if add else ())
    return pl.pallas_call(
        functools.partial(image_kernel, add),
        out_shape=jax.ShapeDtypeStruct(shape, jnp.float32),
        in_specs=[pl.BlockSpec(memory_space=pltpu.VMEM)] * len(args),
        out_specs=pl.BlockSpec(memory_space=pltpu.VMEM),
        compiler_params=pltpu.CompilerParams(vmem_limit_bytes=50 << 20),
    )(*args)


def chip_shards(
    fields, surface, held_freqs, surface_freqs, ref_slowness, weights, regions, region_slowness
):
    lat = lax.axis_size("lat")
    depth = lax.axis_size("depth")
    depth_index = lax.axis_index("depth")
    core = depth_index % 2
    block_index = lax.axis_index("lat")
    place = block_index % 2
    field = block_index // 2
    at_first = core == 0
    freq_count = held_freqs.shape[1]
    field_count = 2 * freq_count
    rows, width = (fields.shape[4], fields.shape[5])
    half = width // 2
    total_rows = rows * lat
    half_lags = LAGS // 2
    swap = [(d, d + 1 - 2 * (d % 2)) for d in range(depth)]
    tables = dft_tables(width)

    def halves(value):
        first, second = (value[..., :half], value[..., half:])
        return (jnp.where(at_first, first, second), jnp.where(at_first, second, first))

    def swapped(value):
        return lax.ppermute(value, "depth", swap)

    def sent(blocks):
        return lax.all_to_all(blocks, "lat", split_axis=0, concat_axis=0, tiled=True)

    def side_by_side(value):
        return jnp.concatenate([value[0], value[1]], axis=-1)

    flat = fields[0].reshape(2, field_count, rows, width)
    own, other = halves(flat)
    own, other = (side_by_side(own), swapped(side_by_side(other)))
    both = jnp.stack(
        [jnp.where(at_first, own, other), jnp.where(at_first, other, own)], axis=1
    ).reshape(lat, rows, width)
    surface_half, _ = halves(surface.reshape(2, field_count, rows, width))
    surface_half = side_by_side(surface_half)
    part = rows // depth
    surface_part = lax.dynamic_slice_in_dim(
        surface_half, depth_index // 2 * (2 * part), 2 * part, axis=1
    ).reshape(lat, part, width)
    held = sent(jnp.concatenate([both, surface_part], axis=1))

    region_ids = jnp.arange(REGIONS, dtype=jnp.int32)
    cell = jnp.zeros((rows, width), jnp.float32)
    for region in range(REGIONS):
        cell = jnp.where(regions[0, 0] == region, region_slowness[0, 0, region], cell)
    numbers = jnp.concatenate(
        [ref_slowness[0, 0], held_freqs[0].astype(jnp.float32) * omega_step]
    )
    other_numbers = swapped(numbers)
    section_numbers = (
        jnp.where(at_first, numbers, other_numbers),
        jnp.where(at_first, other_numbers, numbers),
    )
    first_numbers = jnp.where(place == 0, section_numbers[0], section_numbers[1])
    below_chip = [
        (d * lat + j, (d * lat + j - 1) if j % 2 else ((d - 2) % depth * lat + j + 1))
        for d in range(depth)
        for j in range(lat)
    ]
    second_numbers = lax.ppermute(first_numbers, ("depth", "lat"), below_chip)
    takes_surface = (depth_index // 2 == depth // 2 - 1) & (place == 1)
    freq = field % freq_count
    freq_ids = jnp.arange(freq_count, dtype=jnp.int32)

    def picked(values):
        return jnp.sum(jnp.where(freq_ids == freq, values, 0.0))

    sign = jnp.where(field < freq_count, -1.0, 1.0)
    omega_one = picked(first_numbers[2:])
    omega_two = jnp.where(
        takes_surface, picked(surface_freqs.astype(jnp.float32) * omega_step), omega_one
    )
    numbers_one = jnp.stack([omega_one, sign, first_numbers[0], first_numbers[1]])
    numbers_two = jnp.stack([omega_two, sign, second_numbers[0], second_numbers[1]])
    core_pair = jnp.stack([core, takes_surface.astype(jnp.int32)])

    cells = jnp.stack([weights[0, 0], cell])
    own_cells, other_cells = halves(cells)
    other_cells = swapped(other_cells)
    zero = jnp.where(at_first, own_cells, other_cells)
    one = jnp.where(at_first, other_cells, own_cells)

    def cell_blocks(even, odd):
        pair = jnp.stack([even, odd])
        return jnp.broadcast_to(pair[None], (lat // 2,) + pair.shape).reshape(
            (lat,) + even.shape
        )

    blocks_one, held, numbers_one, numbers_two = lax.optimization_barrier(
        (cell_blocks(zero, one), held, numbers_one, numbers_two)
    )
    cells_one = sent(blocks_one)
    cells_two = lax.ppermute(cells_one, ("depth", "lat"), below_chip)

    last = depth // 2 - 1
    surface_part = held[:, rows:]
    pieces = []
    for piece in range(depth):
        plane, side = (piece // 2, piece % 2)
        if (plane, side) == (last, 1):
            pieces.append(surface_part)
            continue
        route = [
            ((2 * plane + c) * lat + 2 * f + side, (2 * last + c) * lat + 2 * f + 1)
            for c in range(2)
            for f in range(field_count)
        ]
        pieces.append(lax.ppermute(surface_part, ("depth", "lat"), route))

    spread = [(total_rows // 2, width)] * 2
    shifted = [(2, total_rows // 2, width)] * 2
    blocks = (lat, rows + 2 * half_lags, width)
    middle = functools.partial(middle_kernel, 1.0 / (total_rows * width))
    image_shape = (LAGS, rows, width)

    spectrum = [(total_rows // 2, width)] * 2
    mixed = [(2, total_rows, half)] * 2
    keep, send = call(start_kernel, spread, [], core_pair, held, tables)
    send = swapped(send)
    keep, send = call(middle, shifted, spectrum, core_pair, numbers_one, keep, send, tables)
    send = swapped(send)
    result, keep, send = call(
        turn_kernel,
        [blocks] + spread,
        mixed,
        core_pair,
        numbers_one,
        keep,
        send,
        cells_one,
        *pieces,
        tables,
    )
    first_out = sent(result).reshape((field_count, 2) + blocks[1:])
    keep, send = call(
        middle, shifted, spectrum, core_pair, numbers_two, keep, swapped(send), tables
    )
    (result,) = call(
        end_kernel,
        [blocks],
        mixed,
        core_pair,
        numbers_two,
        keep,
        swapped(send),
        cells_two,
        tables,
    )
    second_out = sent(result).reshape((field_count, 2) + blocks[1:])

    mine = jnp.where(at_first, first_out[:, 0], first_out[:, 1])
    theirs = swapped(jnp.where(at_first, first_out[:, 1], first_out[:, 0]))
    image = call_image(
        False,
        jnp.where(at_first, mine, theirs),
        jnp.where(at_first, theirs, mine),
        None,
        image_shape,
    )
    below = lax.ppermute(
        jnp.where(at_first, second_out[:, 0], second_out[:, 1]),
        "depth",
        [(d, (d + 1) % depth) for d in range(depth)],
    )
    down = lax.ppermute(
        second_out[:, 1], "depth", [(d, (d + 2) % depth) for d in range(0, depth, 2)]
    )
    left = jnp.where(at_first, down, below)
    right = jnp.where(at_first, below, second_out[:, 0])
    image = call_image(True, left, right, image, image_shape)
    inner = slice(half_lags, half_lags + rows)
    fields_out = jnp.stack(
        [
            jnp.concatenate([left[:, inner, :half], right[:, inner, :half]], axis=-1),
            jnp.concatenate([left[:, inner, half:], right[:, inner, half:]], axis=-1),
        ]
    ).reshape(fields.shape)
    return (fields_out, image[None, None])


def solution(mesh):
    in_specs = (
        P("depth", None, None, None, "lat", None),
        P(None, None, None, "lat", None),
        P("depth", None),
        P(),
        P("depth", None, None),
        P("depth", None, "lat", None),
        P("depth", None, "lat", None),
        P("depth", None, None),
    )
    out_specs = (P("depth", None, None, None, "lat", None), P("depth", None, None, "lat", None))

    def body(*args):
        fields = args[0]
        one_to_a_chip = lax.axis_size("lat") == 2 * fields.shape[2] * fields.shape[3]
        square = fields.shape[4] * lax.axis_size("lat") == fields.shape[5]
        depth = lax.axis_size("depth")
        if one_to_a_chip and square and depth % 2 == 0 and fields.shape[4] % (8 * depth) == 0:
            return chip_shards(*args)
        return shards(*args)

    return jax.shard_map(body, mesh=mesh, in_specs=in_specs, out_specs=out_specs, check_vma=False)
```
